32 devices in a mesh: pipe: 4 (over y, core), expert: 4 (over z), dp: 2 (over x).
Axes of the slice: x: 2, y: 2, z: 4, core: 2. Of those that a mesh axis runs over, the one named last changes fastest.
Arguments:
- forward_in: bfloat16 [4, 448, 7168], P('pipe', 'expert', 'dp'), may hold values from -6 to 6
- forward_routes: int32 [4, 448, 2], P('pipe', 'expert'), may hold values from 0 to 3, all different within a row; in each aligned block of 112 rows (0 to 111, 112 to 223, ..., all dimensions but the last counted through in order) at most 84 rows name the same one
- forward_gates: bfloat16 [4, 448, 2], P('pipe', 'expert'), may hold values from 0.29882812 to 1.5
- forward_hidden: bfloat16 [4, 448, 2, 1024], P('pipe', 'expert', None, 'dp'), may hold values from -6 to 6
- backward_in: bfloat16 [4, 448, 7168], P('pipe', 'expert', 'dp'), may hold values from -0.14941406 to 0.14941406
- backward_routes: int32 [4, 448, 2], P('pipe', 'expert'), may hold values from 0 to 3, all different within a row; in each aligned block of 112 rows (0 to 111, 112 to 223, ..., all dimensions but the last counted through in order) at most 84 rows name the same one
- backward_gates: bfloat16 [4, 448, 2], P('pipe', 'expert'), may hold values from 0.29882812 to 1.5
- backward_hidden: bfloat16 [4, 448, 2, 1024], P('pipe', 'expert', None, 'dp'), may hold values from -6 to 6
- down_weight: bfloat16 [4, 4, 1024, 7168], P('pipe', 'expert', None, 'dp'), may hold values from -0.1875 to 0.1875
Outputs:
- forward_out: bfloat16 [4, 448, 7168], P('pipe', 'expert', 'dp')
- hidden_grads: bfloat16 [4, 448, 2, 1024], P('pipe', 'expert', None, 'dp')
- gate_grads: bfloat16 [4, 448, 2], P('pipe', 'expert')
The draws below stay inside these ranges and needn't reach their ends.
Inputs may be any that keep to these rules, and one draw needn't show every extreme that they name: `forward_routes`: in each aligned block of 112 tokens (one index of expert at one section) the 2 routes of a token name different experts and no expert is named by more than 84 routes of the block; some block names some expert exactly 84 times. `backward_routes`: in each aligned block of 112 tokens (one index of expert at one section) the 2 routes of a token name different experts and no expert is named by more than 84 routes of the block; some block names some expert exactly 84 times.
All inputs are finite; a program needn't handle non-finite values.
Results may differ from the reference program's by a relative error of at most 0.0042.
Values may be sent and summed in bfloat16 or wider, within the bound.
A program may use at most 64 MiB of HBM per device.

```python
import math
import jax
import jax.numpy as jnp
import numpy as np
from jax import lax

D = 7168
FF = 1024
ROUTES = 2
TOK_DEV = 112
EXPERTS = 4
CAP = 84
TOKENS = 448
N_PIPE = 4
N_EXPERT = 4


def level_of(rng, shape, split, smallest, top_value):
    factor_of = 1.0
    for axis_at, shards_of in split:
        draws = jax.random.uniform(jax.random.fold_in(jax.random.fold_in(rng, 6), axis_at), (shards_of,), jnp.float32, smallest / len(split), top_value / len(split))
        factor_of = factor_of * jnp.repeat(jnp.exp(draws), shape[axis_at] // shards_of).reshape((-1,) + (1,) * (len(shape) - 1 - axis_at))
    return factor_of


def deal_out(key, own, number, rows, number_of, top, limit, slope):
    ranking = jax.random.permutation(key, number_of)
    crowded, common = load_shares(number_of, rows * top, limit, slope, True), load_shares(number_of, rows * top, limit, slope, False)
    places = jnp.arange(number_of)

    def named(lengths, turn):
        used = int((lengths > 0).sum())
        fixed = max(1, used // 4)
        moved = fixed + (places - fixed + turn * (used - fixed)) % max(1, number_of - fixed)
        return jnp.zeros((number_of,), jnp.int32).at[ranking[jnp.where(places < fixed, places, moved)]].set(jnp.asarray(lengths, jnp.int32))

    lengths = jnp.where(number % 4 == 0, named(crowded, number // 4), named(common, number - number // 4 - 1))
    mixed = jax.random.permutation(jax.random.fold_in(own, 3), number_of)
    giver, taker = mixed[0:number_of // 2 * 2:2], mixed[1:number_of // 2 * 2:2]
    room = jnp.minimum(lengths[giver] - 1, limit - lengths[taker]) // 2
    room = jnp.where((giver == ranking[0]) | (taker == ranking[0]) | (lengths[taker] == 0), 0, jnp.maximum(room, 0))
    moved = jax.random.randint(jax.random.fold_in(own, 4), (number_of // 2,), 0, 1 << 20) % (room + 1)
    lengths = lengths.at[giver].add(-moved).at[taker].add(moved)
    members = jnp.searchsorted(jnp.cumsum(lengths), jnp.arange(rows * top), side="right").astype(jnp.int32)
    table = members.reshape(top, rows).T
    table = table[jax.random.permutation(jax.random.fold_in(own, 1), rows)]
    turn = jax.random.randint(jax.random.fold_in(own, 2), (rows, 1), 0, top)
    return jnp.take_along_axis(table, (jnp.arange(top)[None, :] + turn) % top, axis=1)


def load_shares(number_of, total, reach, skew, full):
    loads = [(1 << 20) // math.isqrt(standing ** skew) + 1 for standing in range(1, number_of + 1)]
    largest = reach if full else min(reach, max(-(-total // number_of), total * loads[0] // sum(loads)))
    least = 1 if total - largest >= number_of - 1 else 0
    holding, spare = [largest] + [least] * (number_of - 1), total - largest - least * (number_of - 1)
    while spare > 0:
        movable = [i for i in range(1, number_of) if holding[i] < largest] or [i for i in range(1, number_of) if holding[i] < reach]
        pool, left = sum([loads[i] for i in movable]), spare
        for i in movable:
            addition = min(reach - holding[i], max(1, left * loads[i] // pool), spare)
            holding[i] = holding[i] + addition
            spare = spare - addition
    return np.array(holding)


def scatter_about(stream_key, dims, deviation, limit, split=(), kind=jnp.bfloat16):
    level = level_of(stream_key, dims, split, -0.22, 0.18) if split else 1.0
    result = jax.random.normal(stream_key, dims, jnp.float32) * deviation * level
    return jnp.minimum(jnp.maximum(result, -limit), limit).astype(kind)


def setup_inputs(seed: int = 0) -> dict:
    splits = jax.random.split(jax.random.key(seed), 10)
    forward_in = scatter_about(splits[0], (N_PIPE, TOKENS, D), 1.0, 6.0, ((0, 4), (1, 4), (2, 2)))
    forward_routes_keys = jax.random.split(jax.random.fold_in(splits[1], 1), N_PIPE * TOKENS // TOK_DEV)
    forward_routes_turns = jax.random.permutation(jax.random.fold_in(splits[1], 3), N_PIPE * TOKENS // TOK_DEV)
    forward_routes = jax.vmap(lambda own, number: deal_out(jax.random.fold_in(splits[1], 2), own, number, TOK_DEV, EXPERTS, ROUTES, CAP, 2))(forward_routes_keys, forward_routes_turns).reshape((N_PIPE, TOKENS, ROUTES))
    forward_gates = jnp.clip(0.29882812 + 1.2011719 * jax.random.uniform(splits[2], (N_PIPE, TOKENS, ROUTES), jnp.float32) ** level_of(splits[2], (N_PIPE, TOKENS, ROUTES), ((0, 4), (1, 4)), -0.2, 0.2), 0.29882812, 1.5).astype(jnp.bfloat16)
    forward_hidden = scatter_about(splits[3], (N_PIPE, TOKENS, ROUTES, FF), 1.0, 6.0, ((0, 4), (1, 4), (3, 2)))
    backward_in = scatter_about(splits[4], (N_PIPE, TOKENS, D), 0.025, 0.14941406, ((0, 4), (1, 4), (2, 2)))
    backward_routes_keys = jax.random.split(jax.random.fold_in(splits[5], 1), N_PIPE * TOKENS // TOK_DEV)
    backward_routes_turns = jax.random.permutation(jax.random.fold_in(splits[5], 3), N_PIPE * TOKENS // TOK_DEV)
    backward_routes = jax.vmap(lambda own, number: deal_out(jax.random.fold_in(splits[5], 2), own, number, TOK_DEV, EXPERTS, ROUTES, CAP, 2))(backward_routes_keys, backward_routes_turns).reshape((N_PIPE, TOKENS, ROUTES))
    backward_gates = jnp.clip(0.29882812 + 1.2011719 * jax.random.uniform(splits[6], (N_PIPE, TOKENS, ROUTES), jnp.float32) ** level_of(splits[6], (N_PIPE, TOKENS, ROUTES), ((0, 4), (1, 4)), -0.2, 0.2), 0.29882812, 1.5).astype(jnp.bfloat16)
    backward_hidden = scatter_about(splits[7], (N_PIPE, TOKENS, ROUTES, FF), 1.0, 6.0, ((0, 4), (1, 4), (3, 2)))
    down_weight = scatter_about(splits[8], (N_PIPE, EXPERTS, FF, D), FF ** -0.5, 0.1875, ((0, 4), (1, 4), (3, 2)))
    return dict(forward_in=forward_in, forward_routes=forward_routes, forward_gates=forward_gates, forward_hidden=forward_hidden, backward_in=backward_in, backward_routes=backward_routes, backward_gates=backward_gates, backward_hidden=backward_hidden, down_weight=down_weight)


def place_routes(routes):
    flat_routes = routes.reshape(-1).astype(jnp.int32)
    owner_ids = jnp.arange(EXPERTS, dtype=jnp.int32)
    one_hot = (flat_routes[:, None] == owner_ids[None, :]).astype(jnp.int32)
    before_count = jnp.cumsum(one_hot, axis=0) - one_hot
    slot_pos = jnp.sum(before_count * one_hot, axis=1).astype(jnp.int32)
    return (flat_routes * CAP + slot_pos).astype(jnp.int32)


def fill_slots(values, target):
    empty = jnp.zeros((EXPERTS * CAP,) + values.shape[1:], values.dtype)
    return empty.at[target].set(values)


def to_experts(buffers, tail):
    shaped = buffers.reshape((N_EXPERT, EXPERTS, CAP) + tail)
    order = (1, 0, 2) + tuple(range(3, 3 + len(tail)))
    return shaped.transpose(order).reshape((EXPERTS, N_EXPERT * CAP) + tail)


def from_experts(results, tail):
    shaped = results.reshape((EXPERTS, N_EXPERT, CAP) + tail)
    order = (1, 0, 2) + tuple(range(3, 3 + len(tail)))
    return shaped.transpose(order).reshape((N_EXPERT, EXPERTS * CAP) + tail)


def expert_forward(operands):
    hidden_rows, weight_part = operands
    return jnp.dot(hidden_rows, weight_part, preferred_element_type=jnp.float32).astype(jnp.bfloat16)


def expert_backward(operands):
    grad_rows, hidden_rows, gate_vals, weight_part = operands
    outward = jnp.dot(hidden_rows, weight_part, preferred_element_type=jnp.float32)
    gate_grad = jnp.sum(grad_rows.astype(jnp.float32) * outward, axis=1).astype(jnp.bfloat16)
    projected = jnp.dot(grad_rows, weight_part.T, preferred_element_type=jnp.float32)
    hidden_grad = (gate_vals.astype(jnp.float32)[:, None] * projected).astype(jnp.bfloat16)
    return hidden_grad, gate_grad


def pick_rows(buffers, targets):
    return jax.vmap(lambda buffer, target: buffer[target])(buffers, targets)


def section_pass(inbound_f, f_routes, f_gates, f_hidden, inbound_b, b_routes, b_gates, b_hidden, weights):
    targets_f = jax.vmap(place_routes)(f_routes.reshape(N_EXPERT, TOK_DEV, ROUTES))
    hidden_buf = jax.vmap(fill_slots)(f_hidden.reshape(N_EXPERT, TOK_DEV * ROUTES, FF), targets_f)
    results = lax.map(expert_forward, (to_experts(hidden_buf, (FF,)), weights))
    picked = pick_rows(from_experts(results, (D,)), targets_f)
    picked = picked.reshape(N_EXPERT, TOK_DEV, ROUTES, D).astype(jnp.float32)
    gate_w = f_gates.reshape(N_EXPERT, TOK_DEV, ROUTES, 1).astype(jnp.float32)
    mixed = inbound_f.reshape(N_EXPERT, TOK_DEV, D).astype(jnp.float32) + jnp.sum(gate_w * picked, axis=2)
    mixed = mixed.astype(jnp.bfloat16).reshape(TOKENS, D)
    targets_b = jax.vmap(place_routes)(b_routes.reshape(N_EXPERT, TOK_DEV, ROUTES))
    grad_rows = jnp.repeat(inbound_b.reshape(N_EXPERT, TOK_DEV, D), ROUTES, axis=1)
    grad_buf = jax.vmap(fill_slots)(grad_rows, targets_b)
    hid_buf = jax.vmap(fill_slots)(b_hidden.reshape(N_EXPERT, TOK_DEV * ROUTES, FF), targets_b)
    gate_buf = jax.vmap(fill_slots)(b_gates.reshape(N_EXPERT, TOK_DEV * ROUTES), targets_b)
    hidden_grad, gate_grad = lax.map(expert_backward, (to_experts(grad_buf, (D,)), to_experts(hid_buf, (FF,)), to_experts(gate_buf, ()), weights))
    picked_h = pick_rows(from_experts(hidden_grad, (FF,)), targets_b).reshape(TOKENS, ROUTES, FF)
    picked_g = pick_rows(from_experts(gate_grad, ()), targets_b).reshape(TOKENS, ROUTES)
    return mixed, picked_h, picked_g


def reference(forward_in, forward_routes, forward_gates, forward_hidden, backward_in, backward_routes, backward_gates, backward_hidden, down_weight):
    out_list, hidden_list, gate_list = [], [], []
    for section_index in range(N_PIPE):
        mixed, picked_h, picked_g = section_pass(forward_in[(section_index - 1) % N_PIPE], forward_routes[section_index], forward_gates[section_index], forward_hidden[section_index], backward_in[(section_index + 1) % N_PIPE], backward_routes[section_index], backward_gates[section_index], backward_hidden[section_index], down_weight[section_index])
        out_list.append(mixed)
        hidden_list.append(picked_h)
        gate_list.append(picked_g)
    return jnp.stack(out_list), jnp.stack(hidden_list), jnp.stack(gate_list)
```

```python
import functools
import jax
import jax.numpy as jnp
from jax import lax
from jax.experimental import pallas as pl
from jax.experimental.pallas import tpu as pltpu
from jax.sharding import PartitionSpec as P


def passed_along(value, axis, steps):
    count = lax.axis_size(axis)
    pairs = [(source, (source + steps) % count) for source in range(count)]
    return lax.ppermute(value, axis, pairs)


def route_targets(routes, capacity):
    flat_routes = routes.reshape(-1)
    places = jnp.arange(flat_routes.shape[0], dtype=jnp.int32)
    same_before = (flat_routes[:, None] == flat_routes[None, :]) & (places[None, :] < places[:, None])
    slot_pos = jnp.sum(same_before.astype(jnp.int32), axis=1)
    return flat_routes * capacity + slot_pos


def fill_slots(values, target, total):
    empty = jnp.zeros((total,) + values.shape[1:], values.dtype)
    return empty.at[target].set(values)


def routed_body(
    forward_in,
    forward_routes,
    forward_gates,
    forward_hidden,
    backward_in,
    backward_routes,
    backward_gates,
    backward_hidden,
    down_weight,
):
    owners = lax.axis_size("expert")
    tokens_here = forward_in.shape[1]
    route_count = forward_routes.shape[2]
    capacity = min(tokens_here, max(2, 3 * tokens_here * route_count // (2 * owners)))
    slot_count = owners * capacity
    inbound_forward = passed_along(forward_in, "pipe", 1)[0]
    inbound_backward = passed_along(backward_in, "pipe", -1)[0]
    target_forward = route_targets(forward_routes[0], capacity)
    target_backward = route_targets(backward_routes[0], capacity)
    weight = down_weight[0, 0]
    quarter = forward_hidden.shape[3]
    hidden_fwd, hidden_bwd = (forward_hidden[0], backward_hidden[0])
    send_fwd_hidden = fill_slots(
        hidden_fwd.reshape(tokens_here * route_count, -1), target_forward, slot_count
    )
    send_grads = fill_slots(
        jnp.repeat(inbound_backward, route_count, axis=0), target_backward, slot_count
    )
    send_bwd_hidden = fill_slots(
        hidden_bwd.reshape(tokens_here * route_count, -1), target_backward, slot_count
    )
    send_gates = fill_slots(backward_gates[0].reshape(-1), target_backward, slot_count)
    got_fwd_hidden = lax.all_to_all(
        send_fwd_hidden, "expert", split_axis=0, concat_axis=0, tiled=True
    )
    got_grads, got_bwd_hidden, got_gates = (
        lax.all_to_all(send_grads, "expert", split_axis=0, concat_axis=0, tiled=True),
        lax.all_to_all(send_bwd_hidden, "expert", split_axis=0, concat_axis=0, tiled=True),
        lax.all_to_all(send_gates, "expert", split_axis=0, concat_axis=0, tiled=True),
    )
    full_fwd, full_bwd = (
        lax.all_gather(got_fwd_hidden, "dp", axis=1, tiled=True),
        lax.all_gather(got_bwd_hidden, "dp", axis=1, tiled=True),
    )
    result_cols = jnp.dot(full_fwd, weight, preferred_element_type=jnp.float32).astype(jnp.bfloat16)
    proj_part = lax.dot_general(
        got_grads, weight, (((1,), (1,)), ((), ())), preferred_element_type=jnp.float32
    )
    projected = lax.psum_scatter(proj_part, "dp", scatter_dimension=1, tiled=True)
    outward = jnp.dot(full_bwd, weight, preferred_element_type=jnp.float32)
    gate_part = jnp.sum(got_grads.astype(jnp.float32) * outward, axis=1)
    gate_total = lax.psum(gate_part, "dp")
    hidden_grad = (got_gates.astype(jnp.float32)[:, None] * projected).astype(jnp.bfloat16)
    gate_grad = gate_total.astype(jnp.bfloat16)
    back_result = lax.all_to_all(result_cols, "expert", split_axis=0, concat_axis=0, tiled=True)
    back_hidden, back_gate = (
        lax.all_to_all(hidden_grad, "expert", split_axis=0, concat_axis=0, tiled=True),
        lax.all_to_all(gate_grad, "expert", split_axis=0, concat_axis=0, tiled=True),
    )
    picked_forward = (
        back_result[target_forward].reshape(tokens_here, route_count, -1).astype(jnp.float32)
    )
    gate_values = forward_gates[0].astype(jnp.float32)[:, :, None]
    forward_out = (
        inbound_forward.astype(jnp.float32) + jnp.sum(gate_values * picked_forward, axis=1)
    ).astype(jnp.bfloat16)
    hidden_grads = back_hidden[target_backward].reshape(tokens_here, route_count, quarter)
    gate_grads = back_gate[target_backward].reshape(tokens_here, route_count)
    return (forward_out[None], hidden_grads[None], gate_grads[None])


F32 = jnp.float32
BF16 = jnp.bfloat16
CHUNK = 512


def line_kernel(
    n,
    pipes,
    fin,
    bin_,
    hf,
    hb,
    rf,
    rb,
    gf,
    gb,
    w,
    out,
    hg,
    gg,
    wv,
    ag,
    inb,
    hs,
    hfull,
    res,
    snd,
    rlo,
    rhi,
    acc,
    ps,
    pr,
    pz,
    pret,
    gs,
    gr,
    w_sem,
    sh_s,
    sh_r,
    fi_s,
    fi_r,
    hd_s,
    hd_r,
    hx_s,
    hx_r,
    agu_s,
    agd_s,
    ag_r,
    rs_s,
    lo_r,
    hi_r,
    px_s,
    px_r,
    pz_s,
    pz_r,
    g_s,
    g_r,
):
    me = lax.axis_index("expert")
    pipe = lax.axis_index("pipe")
    half = lax.axis_index("dp")
    other = 1 - half
    after, before = lax.rem(pipe + 1, pipes), lax.rem(pipe + pipes - 1, pipes)
    width = fin.shape[1]
    fl = hs.shape[2]
    chunks = width // CHUNK
    early = chunks // 2

    def cols(c):
        return pl.ds(pl.multiple_of(c * CHUNK, CHUNK), CHUNK)

    def remote(source, target, send, recv, **device):
        return pltpu.make_async_remote_copy(
            src_ref=source,
            dst_ref=target,
            send_sem=send,
            recv_sem=recv,
            device_id=device,
            device_id_type=pl.DeviceIdType.MESH,
        )

    def shift(c):
        return remote(
            bin_.at[:, cols(c)], ag.at[me, :, cols(c)], sh_s.at[c], sh_r.at[c], pipe=before
        )

    def forward_shift():
        return remote(fin, inb, fi_s, fi_r, pipe=after)

    def hidden_to(e):
        return remote(hs.at[e], hfull.at[half, me], hd_s.at[e], hd_r.at[me], expert=e)

    def hidden_from(s):
        return remote(hs.at[s], hfull.at[half, s], hd_s.at[s], hd_r.at[s], expert=s)

    def hidden_across(s):
        return remote(hfull.at[half, s], hfull.at[half, s], hx_s.at[s], hx_r.at[s], dp=other)

    def gather_up(b, c):
        part = ag.at[b, :, cols(c)]
        return remote(part, part, agu_s.at[b, c], ag_r.at[b, c], expert=me + 1)

    def gather_down(b, c):
        part = ag.at[b, :, cols(c)]
        return remote(part, part, agd_s.at[b, c], ag_r.at[b, c], expert=me - 1)

    def sum_up(b, c):
        return remote(
            snd.at[b, :, cols(c)], rlo.at[b, :, cols(c)], rs_s.at[b, c], lo_r.at[b, c], expert=me + 1
        )

    def sum_down(b, c):
        return remote(
            snd.at[b, :, cols(c)], rhi.at[b, :, cols(c)], rs_s.at[b, c], hi_r.at[b, c], expert=me - 1
        )

    def proj_across(b):
        return remote(ps.at[b], pr.at[b], px_s.at[b], px_r.at[b], dp=other)

    def proj_to(b):
        return remote(pz.at[b], pret.at[me], pz_s.at[b], pz_r.at[me], expert=b)

    def proj_from(e):
        return remote(pz.at[e], pret.at[e], pz_s.at[e], pz_r.at[e], expert=e)

    def gate_across():
        return remote(gs, gr, g_s, g_r, dp=other)

    load_w = pltpu.make_async_copy(w, wv, w_sem)
    load_w.start()

    barrier = pltpu.get_barrier_semaphore()
    for device in ({"pipe": after}, {"pipe": before}, {"dp": other}):
        pl.semaphore_signal(
            barrier, inc=1, device_id=device, device_id_type=pl.DeviceIdType.MESH
        )
    for step in range(1, n):
        pl.semaphore_signal(
            barrier,
            inc=1,
            device_id={"expert": lax.rem(me + step, n)},
            device_id_type=pl.DeviceIdType.MESH,
        )
    pl.semaphore_wait(barrier, 3 + n - 1)

    def each_chunk(action):
        lax.fori_loop(0, chunks, lambda c, _: (action(c), 0)[1], 0)

    each_chunk(lambda c: shift(c).start())

    table = jnp.concatenate(
        [rf[...].astype(F32), gf[...].astype(F32), rb[...].astype(F32), gb[...].astype(F32)], axis=0
    ).T
    h0 = hf[:, 0, :].astype(F32) * table[:, 2:3]
    h1 = hf[:, 1, :].astype(F32) * table[:, 3:4]

    def weighted(e):
        name = lax.convert_element_type(e, F32)
        return (
            jnp.where(table[:, 0:1] == name, h0, 0.0) + jnp.where(table[:, 1:2] == name, h1, 0.0)
        ).astype(BF16)

    for step in range(1, n):
        e = lax.rem(me + step, n)
        hs[e] = weighted(e)
        hidden_to(e).start()
    hfull[half, me] = weighted(me)
    hidden_across(me).start()

    def own_chunk(c):
        shift(c).wait_recv()

        @pl.when(me < n - 1)
        def _():
            gather_up(me, c).start()

        @pl.when(me > 0)
        def _():
            gather_down(me, c).start()

    each_chunk(own_chunk)
    forward_shift().start()

    for step in range(1, n):
        s = lax.rem(me + step, n)
        hidden_from(s).wait_recv()
        hidden_across(s).start()
    load_w.wait()
    for step in range(n):
        hidden_across(lax.rem(me + step, n)).wait_recv()

    rows = hfull.shape[2]

    def expert_chunk(c):
        left = hfull[0].reshape(n * rows, fl)
        right = hfull[1].reshape(n * rows, fl)
        got = jnp.dot(left, wv[:fl, cols(c)], preferred_element_type=F32)
        got = got + jnp.dot(right, wv[fl:, cols(c)], preferred_element_type=F32)
        res[:, :, cols(c)] = got.reshape(n, rows, CHUNK)

    each_chunk(expert_chunk)

    def first_sums(far, c):
        @pl.when(me == 0)
        def _():
            snd[far, :, cols(c)] = res[far, :, cols(c)].astype(BF16)
            sum_up(far, c).start()

        @pl.when(me == n - 1)
        def _():
            near = n - 1 - far
            snd[near, :, cols(c)] = res[near, :, cols(c)].astype(BF16)
            sum_down(near, c).start()

    each_chunk(lambda c: first_sums(n - 1, c))

    def project(b, c):
        grads = ag[b, :, cols(c)]
        for part in range(2):
            got = lax.dot_general(
                grads,
                wv[part * fl : (part + 1) * fl, cols(c)],
                (((1,), (1,)), ((), ())),
                preferred_element_type=F32,
            )

            @pl.when(c == 0)
            def _():
                acc[part, b] = got

            @pl.when(c > 0)
            def _():
                acc[part, b] = acc[part, b] + got

    def to_peer(b):
        ps[b] = acc[other, b].astype(BF16)
        proj_across(b).start()

    def to_source(b):
        proj_across(b).wait_recv()
        pz[b] = (acc[half, b] + pr[b].astype(F32)).astype(BF16)
        proj_to(b).start()

    def window(step):
        low, high = me - step, me + step
        up_to, down_to = me + n - step, me - (n - step)
        from_low, from_high = low >= 0, high < n

        def chunk(c):
            @pl.when(from_low)
            def _():
                gather_up(low, c).wait_recv()

                @pl.when(me < n - 1)
                def _():
                    gather_up(low, c).start()

            @pl.when(from_high)
            def _():
                gather_down(high, c).wait_recv()

                @pl.when(me > 0)
                def _():
                    gather_down(high, c).start()

            if 2 <= step < n - 1:
                first_sums(n - step, c)
            elif step == n - 1:

                @pl.when(c < early)
                def _():
                    first_sums(1, c)

            if step >= 2:

                @pl.when((me >= 1) & (up_to < n))
                def _():
                    sum_up(up_to, c).wait_recv()
                    snd[up_to, :, cols(c)] = (
                        res[up_to, :, cols(c)] + rlo[up_to, :, cols(c)].astype(F32)
                    ).astype(BF16)
                    sum_up(up_to, c).start()

                @pl.when((me < n - 1) & (down_to >= 0))
                def _():
                    sum_down(down_to, c).wait_recv()
                    snd[down_to, :, cols(c)] = (
                        res[down_to, :, cols(c)] + rhi[down_to, :, cols(c)].astype(F32)
                    ).astype(BF16)
                    sum_down(down_to, c).start()

            @pl.when(from_low)
            def _():
                project(low, c)

            @pl.when(from_high)
            def _():
                project(high, c)

            if step == 1:
                project(me, c)

        lax.fori_loop(0, early, lambda c, _: (chunk(c), 0)[1], 0)
        if step >= 2:
            hand_back(step - 1)
        lax.fori_loop(early, chunks, lambda c, _: (chunk(c), 0)[1], 0)

        @pl.when(from_low)
        def _():
            to_peer(low)

        @pl.when(from_high)
        def _():
            to_peer(high)

        if step == 1:
            to_peer(me)

    def hand_back(step):
        low, high = me - step, me + step

        @pl.when(low >= 0)
        def _():
            to_source(low)

        @pl.when(high < n)
        def _():
            to_source(high)

    for step in range(1, n):
        window(step)
    hand_back(n - 1)
    lax.fori_loop(early, chunks, lambda c, _: (first_sums(1, c), 0)[1], 0)
    proj_across(me).wait_recv()
    pret[me] = (acc[half, me] + pr[me].astype(F32)).astype(BF16)

    for step in range(1, n):
        proj_from(lax.rem(me + step, n)).wait_recv()
    lane = lax.broadcasted_iota(jnp.int32, gs.shape, 1)
    gate_sum = jnp.zeros(gs.shape, F32)
    for k in range(2):
        picked = jnp.zeros((rows, fl), F32)
        for e in range(n):
            picked = picked + jnp.where(
                table[:, 4 + k : 5 + k] == float(e), pret[e].astype(F32), 0.0
            )
        hg[:, k, :] = (table[:, 6 + k : 7 + k] * picked).astype(BF16)
        part = jnp.sum(hb[:, k, :].astype(F32) * picked, axis=1, keepdims=True)
        gate_sum = gate_sum + jnp.where(lane == k, part, 0.0)
    gs[...] = gate_sum
    gate_across().start()

    forward_shift().wait_recv()

    def final_chunk(c):
        def total(value):
            out[:, cols(c)] = value.astype(BF16)

        base = inb[:, cols(c)].astype(F32) + res[me, :, cols(c)]

        @pl.when(me > 0)
        def _():
            sum_up(me, c).wait_recv()

        @pl.when(me < n - 1)
        def _():
            sum_down(me, c).wait_recv()

        @pl.when(me == 0)
        def _():
            total(base + rhi[me, :, cols(c)].astype(F32))

        @pl.when(me == n - 1)
        def _():
            total(base + rlo[me, :, cols(c)].astype(F32))

        @pl.when((me > 0) & (me < n - 1))
        def _():
            total(
                base + rlo[me, :, cols(c)].astype(F32) + rhi[me, :, cols(c)].astype(F32)
            )

    each_chunk(final_chunk)
    gate_across().wait_recv()
    gg[...] = (gs[...] + gr[...]).T[:2].astype(BF16)

    each_chunk(lambda c: shift(c).wait_send())
    forward_shift().wait_send()
    for step in range(1, n):
        e = lax.rem(me + step, n)
        hidden_to(e).wait_send()
        proj_to(e).wait_send()
    for b in range(n):
        hidden_across(b).wait_send()
        proj_across(b).wait_send()

        def drain(c):
            @pl.when((b <= me) & (me < n - 1))
            def _():
                gather_up(b, c).wait_send()

            @pl.when((b >= me) & (me > 0))
            def _():
                gather_down(b, c).wait_send()

            @pl.when(b != me)
            def _():
                sum_up(b, c).wait_send()

        each_chunk(drain)
    gate_across().wait_send()


def store_kernel(out_v, hg_v, gg_v, out, hg, gg, sems):
    copies = [
        pltpu.make_async_copy(source, target, sems.at[i])
        for i, (source, target) in enumerate(((out_v, out), (hg_v, hg), (gg_v, gg)))
    ]
    for copy in copies:
        copy.start()
    for copy in copies:
        copy.wait()


def line_body(
    forward_in,
    forward_routes,
    forward_gates,
    forward_hidden,
    backward_in,
    backward_routes,
    backward_gates,
    backward_hidden,
    down_weight,
):
    n = lax.axis_size("expert")
    pipes = lax.axis_size("pipe")
    rows, width = forward_in.shape[1:]
    top, fl = forward_hidden.shape[2:]
    chunks = width // CHUNK
    dma = pltpu.SemaphoreType.DMA
    vmem = pl.BlockSpec(memory_space=pltpu.VMEM)
    hbm = pl.BlockSpec(memory_space=pl.ANY)
    block = pltpu.VMEM((n, rows, width), BF16)
    small = pltpu.VMEM((n, rows, fl), BF16)
    gate_tile = pltpu.VMEM((rows, 128), F32)
    out, hidden_grads, gate_grads = pl.pallas_call(
        functools.partial(line_kernel, n, pipes),
        out_shape=(
            pltpu.VMEM((rows, width), BF16),
            pltpu.VMEM((rows, top, fl), BF16),
            pltpu.VMEM((top, rows), BF16),
        ),
        in_specs=[hbm, hbm] + [vmem] * 6 + [hbm],
        out_specs=(vmem, vmem, vmem),
        scratch_shapes=[
            pltpu.VMEM((2 * fl, width), BF16),
            block,
            pltpu.VMEM((rows, width), BF16),
            small,
            pltpu.VMEM((2, n, rows, fl), BF16),
            pltpu.VMEM((n, rows, width), F32),
            block,
            block,
            block,
            pltpu.VMEM((2, n, rows, fl), F32),
            small,
            small,
            small,
            small,
            gate_tile,
            gate_tile,
            dma,
            dma((chunks,)),
            dma((chunks,)),
            dma,
            dma,
            dma((n,)),
            dma((n,)),
            dma((n,)),
            dma((n,)),
            dma((n, chunks)),
            dma((n, chunks)),
            dma((n, chunks)),
            dma((n, chunks)),
            dma((n, chunks)),
            dma((n, chunks)),
            dma((n,)),
            dma((n,)),
            dma((n,)),
            dma((n,)),
            dma,
            dma,
        ],
        compiler_params=pltpu.CompilerParams(
            collective_id=0, has_side_effects=True, vmem_limit_bytes=56 << 20
        ),
    )(
        forward_in[0],
        backward_in[0],
        forward_hidden[0],
        backward_hidden[0],
        forward_routes[0].T,
        backward_routes[0].T,
        forward_gates[0].T,
        backward_gates[0].T,
        down_weight[0, 0],
    )
    out, hidden_grads, gate_grads = pl.pallas_call(
        store_kernel,
        out_shape=(
            jax.ShapeDtypeStruct((rows, width), BF16),
            jax.ShapeDtypeStruct((rows, top, fl), BF16),
            jax.ShapeDtypeStruct((top, rows), BF16),
        ),
        in_specs=[vmem] * 3,
        out_specs=(hbm,) * 3,
        scratch_shapes=[dma((3,))],
    )(
        *(pltpu.with_memory_space_constraint(value, pltpu.VMEM) for value in (out, hidden_grads, gate_grads))
    )
    return out[None], hidden_grads[None], gate_grads.T[None]


def solution(mesh):
    return jax.shard_map(
        line_body if mesh.shape["expert"] <= 4 and mesh.shape["dp"] == 2 else routed_body,
        mesh=mesh,
        in_specs=(
            P("pipe", "expert", "dp"),
            P("pipe", "expert", None),
            P("pipe", "expert", None),
            P("pipe", "expert", None, "dp"),
            P("pipe", "expert", "dp"),
            P("pipe", "expert", None),
            P("pipe", "expert", None),
            P("pipe", "expert", None, "dp"),
            P("pipe", "expert", None, "dp"),
        ),
        out_specs=(
            P("pipe", "expert", "dp"),
            P("pipe", "expert", None, "dp"),
            P("pipe", "expert", None),
        ),
        check_vma=False,
    )
```

```python
import functools
import jax
import jax.numpy as jnp
from jax import lax
from jax.experimental import pallas as pl
from jax.experimental.pallas import tpu as pltpu
from jax.sharding import PartitionSpec as P


def passed_along(value, axis, steps):
    count = lax.axis_size(axis)
    pairs = [(source, (source + steps) % count) for source in range(count)]
    return lax.ppermute(value, axis, pairs)


def route_targets(routes, capacity):
    flat_routes = routes.reshape(-1)
    places = jnp.arange(flat_routes.shape[0], dtype=jnp.int32)
    same_before = (flat_routes[:, None] == flat_routes[None, :]) & (places[None, :] < places[:, None])
    slot_pos = jnp.sum(same_before.astype(jnp.int32), axis=1)
    return flat_routes * capacity + slot_pos


def fill_slots(values, target, total):
    empty = jnp.zeros((total,) + values.shape[1:], values.dtype)
    return empty.at[target].set(values)


def routed_body(
    forward_in,
    forward_routes,
    forward_gates,
    forward_hidden,
    backward_in,
    backward_routes,
    backward_gates,
    backward_hidden,
    down_weight,
):
    owners = lax.axis_size("expert")
    tokens_here = forward_in.shape[1]
    route_count = forward_routes.shape[2]
    capacity = min(tokens_here, max(2, 3 * tokens_here * route_count // (2 * owners)))
    slot_count = owners * capacity
    inbound_forward = passed_along(forward_in, "pipe", 1)[0]
    inbound_backward = passed_along(backward_in, "pipe", -1)[0]
    target_forward = route_targets(forward_routes[0], capacity)
    target_backward = route_targets(backward_routes[0], capacity)
    weight = down_weight[0, 0]
    quarter = forward_hidden.shape[3]
    hidden_fwd, hidden_bwd = (forward_hidden[0], backward_hidden[0])
    send_fwd_hidden = fill_slots(
        hidden_fwd.reshape(tokens_here * route_count, -1), target_forward, slot_count
    )
    send_grads = fill_slots(
        jnp.repeat(inbound_backward, route_count, axis=0), target_backward, slot_count
    )
    send_bwd_hidden = fill_slots(
        hidden_bwd.reshape(tokens_here * route_count, -1), target_backward, slot_count
    )
    send_gates = fill_slots(backward_gates[0].reshape(-1), target_backward, slot_count)
    got_fwd_hidden = lax.all_to_all(
        send_fwd_hidden, "expert", split_axis=0, concat_axis=0, tiled=True
    )
    got_grads, got_bwd_hidden, got_gates = (
        lax.all_to_all(send_grads, "expert", split_axis=0, concat_axis=0, tiled=True),
        lax.all_to_all(send_bwd_hidden, "expert", split_axis=0, concat_axis=0, tiled=True),
        lax.all_to_all(send_gates, "expert", split_axis=0, concat_axis=0, tiled=True),
    )
    full_fwd, full_bwd = (
        lax.all_gather(got_fwd_hidden, "dp", axis=1, tiled=True),
        lax.all_gather(got_bwd_hidden, "dp", axis=1, tiled=True),
    )
    result_cols = jnp.dot(full_fwd, weight, preferred_element_type=jnp.float32).astype(jnp.bfloat16)
    proj_part = lax.dot_general(
        got_grads, weight, (((1,), (1,)), ((), ())), preferred_element_type=jnp.float32
    )
    projected = lax.psum_scatter(proj_part, "dp", scatter_dimension=1, tiled=True)
    outward = jnp.dot(full_bwd, weight, preferred_element_type=jnp.float32)
    gate_part = jnp.sum(got_grads.astype(jnp.float32) * outward, axis=1)
    gate_total = lax.psum(gate_part, "dp")
    hidden_grad = (got_gates.astype(jnp.float32)[:, None] * projected).astype(jnp.bfloat16)
    gate_grad = gate_total.astype(jnp.bfloat16)
    back_result = lax.all_to_all(result_cols, "expert", split_axis=0, concat_axis=0, tiled=True)
    back_hidden, back_gate = (
        lax.all_to_all(hidden_grad, "expert", split_axis=0, concat_axis=0, tiled=True),
        lax.all_to_all(gate_grad, "expert", split_axis=0, concat_axis=0, tiled=True),
    )
    picked_forward = (
        back_result[target_forward].reshape(tokens_here, route_count, -1).astype(jnp.float32)
    )
    gate_values = forward_gates[0].astype(jnp.float32)[:, :, None]
    forward_out = (
        inbound_forward.astype(jnp.float32) + jnp.sum(gate_values * picked_forward, axis=1)
    ).astype(jnp.bfloat16)
    hidden_grads = back_hidden[target_backward].reshape(tokens_here, route_count, quarter)
    gate_grads = back_gate[target_backward].reshape(tokens_here, route_count)
    return (forward_out[None], hidden_grads[None], gate_grads[None])


F32 = jnp.float32
BF16 = jnp.bfloat16
CHUNK = 1792


def line_kernel(
    n,
    pipes,
    capacity,
    fin,
    bin_,
    hf,
    hb,
    rf,
    rb,
    gf,
    gb,
    w,
    out,
    hg,
    gg,
    hfv,
    hbv,
    rfv,
    rbv,
    gfv,
    gbv,
    wv,
    ag,
    inb,
    hs,
    hrecv,
    slot_rows,
    hfull,
    res,
    snd,
    rlo,
    rhi,
    acc,
    ps,
    pr,
    pz,
    pret,
    gs,
    gr,
    in_sem,
    sh_s,
    sh_r,
    fi_s,
    fi_r,
    hd_s,
    hd_r,
    hx_s,
    hx_r,
    agu_s,
    agd_s,
    ag_r,
    rs_s,
    lo_r,
    hi_r,
    px_s,
    px_r,
    pz_s,
    pz_r,
    g_s,
    g_r,
):
    me = lax.axis_index("expert")
    pipe = lax.axis_index("pipe")
    half = lax.axis_index("dp")
    other = 1 - half
    after, before = lax.rem(pipe + 1, pipes), lax.rem(pipe + pipes - 1, pipes)
    rows, width = fin.shape
    fl = hf.shape[2]
    chunks = width // CHUNK
    early = chunks // 2
    packed, lanes = hs.shape[1:]
    slots = packed // 2

    def cols(c):
        return pl.ds(pl.multiple_of(c * CHUNK, CHUNK), CHUNK)

    def remote(source, target, send, recv, **device):
        return pltpu.make_async_remote_copy(
            src_ref=source,
            dst_ref=target,
            send_sem=send,
            recv_sem=recv,
            device_id=device,
            device_id_type=pl.DeviceIdType.MESH,
        )

    def shift(c):
        return remote(bin_.at[:, cols(c)], ag.at[me, c], sh_s.at[c], sh_r.at[c], pipe=before)

    def forward_shift():
        return remote(fin, inb, fi_s, fi_r, pipe=after)

    def hidden_to(e):
        return remote(hs.at[e], hrecv.at[half, me], hd_s.at[e], hd_r.at[me], expert=e)

    def hidden_from(s):
        return remote(hs.at[s], hrecv.at[half, s], hd_s.at[s], hd_r.at[s], expert=s)

    def hidden_across(s):
        part = hrecv.at[half, s]
        return remote(part, part, hx_s.at[s], hx_r.at[s], dp=other)

    def gather_up(b, c):
        part = ag.at[b, c]
        return remote(part, part, agu_s.at[b, c], ag_r.at[b, c], expert=me + 1)

    def gather_down(b, c):
        part = ag.at[b, c]
        return remote(part, part, agd_s.at[b, c], ag_r.at[b, c], expert=me - 1)

    def sum_up(b, c):
        return remote(snd.at[b, c], rlo.at[b, c], rs_s.at[b, c], lo_r.at[b, c], expert=me + 1)

    def sum_down(b, c):
        return remote(snd.at[b, c], rhi.at[b, c], rs_s.at[b, c], hi_r.at[b, c], expert=me - 1)

    def proj_across(b):
        return remote(ps.at[b], pr.at[b], px_s.at[b], px_r.at[b], dp=other)

    def proj_to(b):
        return remote(pz.at[b], pret.at[me], pz_s.at[b], pz_r.at[me], expert=b)

    def proj_from(e):
        return remote(pz.at[e], pret.at[e], pz_s.at[e], pz_r.at[e], expert=e)

    def gate_across():
        return remote(gs, gr, g_s, g_r, dp=other)

    loads = [
        pltpu.make_async_copy(source, target, in_sem.at[i])
        for i, (source, target) in enumerate(
            ((rf, rfv), (rb, rbv), (gf, gfv), (gb, gbv), (hf, hfv), (hb, hbv), (w, wv))
        )
    ]
    for load in loads:
        load.start()

    barrier = pltpu.get_barrier_semaphore()
    for device in ({"pipe": after}, {"pipe": before}, {"dp": other}):
        pl.semaphore_signal(
            barrier, inc=1, device_id=device, device_id_type=pl.DeviceIdType.MESH
        )
    for step in range(1, n):
        pl.semaphore_signal(
            barrier,
            inc=1,
            device_id={"expert": lax.rem(me + step, n)},
            device_id_type=pl.DeviceIdType.MESH,
        )

    def each_chunk(action):
        lax.fori_loop(0, chunks, lambda c, _: (action(c), 0)[1], 0)

    def pack(value):
        return jnp.concatenate([value[:, :lanes], value[:, lanes:]], axis=0).astype(BF16)

    def unpack(value):
        value = value.astype(F32)
        return jnp.concatenate([value[:slots], value[slots:]], axis=1)

    for load in loads[:4]:
        load.wait()
    fwd, bwd = rfv[...].astype(F32), rbv[...].astype(F32)
    at_row = lax.broadcasted_iota(jnp.int32, (2 * n, rows), 0)
    name = jnp.where(at_row >= n, at_row - n, at_row).astype(F32)
    named = jnp.zeros((2 * n, rows), F32)
    for k in range(2):
        route = jnp.where(at_row >= n, bwd[k : k + 1], fwd[k : k + 1])
        named = named + jnp.where(route == name, 1.0, 0.0)
    earlier = lax.broadcasted_iota(jnp.int32, (rows, rows), 0)
    earlier = jnp.where(earlier < lax.broadcasted_iota(jnp.int32, (rows, rows), 1), 1.0, 0.0)
    count = jnp.dot(named.astype(BF16), earlier.astype(BF16), preferred_element_type=F32)
    slot = jnp.where(named > 0.0, count, -1.0)
    diagonal = lax.broadcasted_iota(jnp.int32, (rows, fl), 0)
    diagonal = jnp.where(diagonal == lax.broadcasted_iota(jnp.int32, (rows, fl), 1), 1.0, 0.0)
    slot_wide = jnp.dot(slot.astype(BF16), diagonal.astype(BF16), preferred_element_type=F32)
    table = jnp.concatenate(
        [fwd, gfv[...].astype(F32), bwd, gbv[...].astype(F32), slot], axis=0
    ).T
    at_slot = lax.broadcasted_iota(jnp.int32, (slots, rows), 0).astype(F32)
    line = lax.broadcasted_iota(jnp.int32, (slots, fl), 0)
    loads[4].wait()
    compact = jnp.zeros((n * slots, fl), F32)
    for k in range(2):
        place = jnp.concatenate(
            [
                jnp.where(
                    (slot[e : e + 1] == at_slot) & (fwd[k : k + 1] == float(e)), 1.0, 0.0
                )
                for e in range(n)
            ],
            axis=0,
        )
        scaled = hfv[:, k, :].astype(F32) * table[:, 2 + k : 3 + k]
        compact = compact + jnp.dot(
            place.astype(BF16), scaled.astype(BF16), preferred_element_type=F32
        )
    for e in range(n):
        piece = compact[e * slots : (e + 1) * slots]
        piece = jnp.where(line == capacity, slot_wide[e : e + 1], piece)
        piece = jnp.where(line == capacity + 1, slot_wide[n + e : n + e + 1], piece)
        hs[e] = pack(piece)

    pl.semaphore_wait(barrier, 3 + n - 1)

    for step in range(1, n):
        hidden_to(lax.rem(me + step, n)).start()
    each_chunk(lambda c: shift(c).start())
    hrecv[half, me] = hs[me]
    hidden_across(me).start()

    def own_chunk(c):
        shift(c).wait_recv()

        @pl.when(me < n - 1)
        def _():
            gather_up(me, c).start()

        @pl.when(me > 0)
        def _():
            gather_down(me, c).start()

    each_chunk(own_chunk)
    forward_shift().start()

    for step in range(1, n):
        s = lax.rem(me + step, n)
        hidden_from(s).wait_recv()
        hidden_across(s).start()

    first_line = slots - 8
    at_lane = lax.broadcasted_iota(jnp.int32, (rows, slots), 1).astype(F32)
    for step in range(n):
        s = lax.rem(me + step, n)
        hidden_across(s).wait_recv()
        mine, theirs = unpack(hrecv[half, s]), unpack(hrecv[other, s])
        lines = mine[first_line:, :rows]
        slot_rows[s, :, :rows] = lines
        column = lines.T[:, capacity - first_line : capacity - first_line + 1]
        spread = jnp.where(column == at_lane, 1.0, 0.0).astype(BF16)
        hfull[half, s] = jnp.dot(
            spread, mine.astype(BF16), preferred_element_type=F32
        ).astype(BF16)
        hfull[other, s] = jnp.dot(
            spread, theirs.astype(BF16), preferred_element_type=F32
        ).astype(BF16)
    loads[6].wait()

    def expert_chunk(c):
        left = hfull[0].reshape(n * rows, fl)
        right = hfull[1].reshape(n * rows, fl)
        got = jnp.dot(left, wv[:fl, cols(c)], preferred_element_type=F32)
        got = got + jnp.dot(right, wv[fl:, cols(c)], preferred_element_type=F32)
        res[:, c] = got.reshape(n, rows, CHUNK)

    each_chunk(expert_chunk)

    def first_sums(far, c):
        @pl.when(me == 0)
        def _():
            snd[far, c] = res[far, c].astype(BF16)
            sum_up(far, c).start()

        @pl.when(me == n - 1)
        def _():
            near = n - 1 - far
            snd[near, c] = res[near, c].astype(BF16)
            sum_down(near, c).start()

    each_chunk(lambda c: first_sums(n - 1, c))

    def project(b, c):
        grads = ag[b, c]
        for part in range(2):
            got = lax.dot_general(
                grads,
                wv[part * fl : (part + 1) * fl, cols(c)],
                (((1,), (1,)), ((), ())),
                preferred_element_type=F32,
            )

            @pl.when(c == 0)
            def _():
                acc[part, b] = got

            @pl.when(c > 0)
            def _():
                acc[part, b] = acc[part, b] + got

    def to_peer(b):
        ps[b] = acc[other, b].astype(BF16)
        proj_across(b).start()

    def gathered(b):
        dense = (acc[half, b] + pr[b].astype(F32)).astype(BF16)
        at = capacity + 1 - first_line
        place = jnp.where(slot_rows[b, at : at + 1, :rows] == at_slot, 1.0, 0.0)
        return pack(jnp.dot(place.astype(BF16), dense, preferred_element_type=F32))

    def to_source(b):
        proj_across(b).wait_recv()
        pz[b] = gathered(b)
        proj_to(b).start()

    def window(step):
        low, high = me - step, me + step
        up_to, down_to = me + n - step, me - (n - step)
        from_low, from_high = low >= 0, high < n

        def chunk(c):
            @pl.when(from_low)
            def _():
                gather_up(low, c).wait_recv()

                @pl.when(me < n - 1)
                def _():
                    gather_up(low, c).start()

            @pl.when(from_high)
            def _():
                gather_down(high, c).wait_recv()

                @pl.when(me > 0)
                def _():
                    gather_down(high, c).start()

            if 2 <= step < n - 1:
                first_sums(n - step, c)
            elif step == n - 1:

                @pl.when(c < early)
                def _():
                    first_sums(1, c)

            if step >= 2:

                @pl.when((me >= 1) & (up_to < n))
                def _():
                    sum_up(up_to, c).wait_recv()
                    snd[up_to, c] = (res[up_to, c] + rlo[up_to, c].astype(F32)).astype(BF16)
                    sum_up(up_to, c).start()

                @pl.when((me < n - 1) & (down_to >= 0))
                def _():
                    sum_down(down_to, c).wait_recv()
                    snd[down_to, c] = (res[down_to, c] + rhi[down_to, c].astype(F32)).astype(BF16)
                    sum_down(down_to, c).start()

            @pl.when(from_low)
            def _():
                project(low, c)

            @pl.when(from_high)
            def _():
                project(high, c)

            if step == 1:
                project(me, c)

        lax.fori_loop(0, early, lambda c, _: (chunk(c), 0)[1], 0)
        if step >= 2:
            hand_back(step - 1)
        lax.fori_loop(early, chunks, lambda c, _: (chunk(c), 0)[1], 0)

        @pl.when(from_low)
        def _():
            to_peer(low)

        @pl.when(from_high)
        def _():
            to_peer(high)

        if step == 1:
            to_peer(me)

    def hand_back(step):
        low, high = me - step, me + step

        @pl.when(low >= 0)
        def _():
            to_source(low)

        @pl.when(high < n)
        def _():
            to_source(high)

    for step in range(1, n):
        window(step)
    hand_back(n - 1)
    lax.fori_loop(early, chunks, lambda c, _: (first_sums(1, c), 0)[1], 0)
    proj_across(me).wait_recv()
    pret[me] = gathered(me)

    for step in range(1, n):
        proj_from(lax.rem(me + step, n)).wait_recv()
    loads[5].wait()
    spreads = [jnp.zeros((rows, fl), F32)] * 2
    for e in range(n):
        spread = jnp.where(table[:, 8 + n + e : 9 + n + e] == at_lane, 1.0, 0.0)
        dense = jnp.dot(
            spread.astype(BF16), unpack(pret[e]).astype(BF16), preferred_element_type=F32
        )
        spreads = [
            total + jnp.where(table[:, 4 + k : 5 + k] == float(e), dense, 0.0)
            for k, total in enumerate(spreads)
        ]
    lane = lax.broadcasted_iota(jnp.int32, gs.shape, 1)
    gate_sum = jnp.zeros(gs.shape, F32)
    for k, picked in enumerate(spreads):
        hg[:, k, :] = (table[:, 6 + k : 7 + k] * picked).astype(BF16)
        part = jnp.sum(hbv[:, k, :].astype(F32) * picked, axis=1, keepdims=True)
        gate_sum = gate_sum + jnp.where(lane == k, part, 0.0)
    gs[...] = gate_sum
    gate_across().start()

    forward_shift().wait_recv()

    def final_chunk(c):
        def total(value):
            out[:, cols(c)] = value.astype(BF16)

        base = inb[:, cols(c)].astype(F32) + res[me, c]

        @pl.when(me > 0)
        def _():
            sum_up(me, c).wait_recv()

        @pl.when(me < n - 1)
        def _():
            sum_down(me, c).wait_recv()

        @pl.when(me == 0)
        def _():
            total(base + rhi[me, c].astype(F32))

        @pl.when(me == n - 1)
        def _():
            total(base + rlo[me, c].astype(F32))

        @pl.when((me > 0) & (me < n - 1))
        def _():
            total(base + rlo[me, c].astype(F32) + rhi[me, c].astype(F32))

    each_chunk(final_chunk)
    gate_across().wait_recv()
    gg[...] = (gs[...] + gr[...]).T[:2].astype(BF16)

    each_chunk(lambda c: shift(c).wait_send())
    forward_shift().wait_send()
    for step in range(1, n):
        e = lax.rem(me + step, n)
        hidden_to(e).wait_send()
        proj_to(e).wait_send()
    for b in range(n):
        hidden_across(b).wait_send()
        proj_across(b).wait_send()

        def drain(c):
            @pl.when((b <= me) & (me < n - 1))
            def _():
                gather_up(b, c).wait_send()

            @pl.when((b >= me) & (me > 0))
            def _():
                gather_down(b, c).wait_send()

            @pl.when(b != me)
            def _():
                sum_up(b, c).wait_send()

        each_chunk(drain)
    gate_across().wait_send()


def store_kernel(out_v, hg_v, gg_v, out, hg, gg, sems):
    copies = [
        pltpu.make_async_copy(source, target, sems.at[i])
        for i, (source, target) in enumerate(((out_v, out), (hg_v, hg), (gg_v, gg)))
    ]
    for copy in copies:
        copy.start()
    for copy in copies:
        copy.wait()


def line_body(
    forward_in,
    forward_routes,
    forward_gates,
    forward_hidden,
    backward_in,
    backward_routes,
    backward_gates,
    backward_hidden,
    down_weight,
):
    n = lax.axis_size("expert")
    pipes = lax.axis_size("pipe")
    rows, width = forward_in.shape[1:]
    top, fl = forward_hidden.shape[2:]
    chunks = width // CHUNK
    capacity = min(rows, max(2, 3 * rows * top // (2 * n)))
    slots = -(-(capacity + 2) // 8) * 8
    dma = pltpu.SemaphoreType.DMA
    vmem = pl.BlockSpec(memory_space=pltpu.VMEM)
    hbm = pl.BlockSpec(memory_space=pl.ANY)
    block = pltpu.VMEM((n, chunks, rows, CHUNK), BF16)
    small = pltpu.VMEM((n, rows, fl), BF16)
    pieces = pltpu.VMEM((n, 2 * slots, fl // 2), BF16)
    gate_tile = pltpu.VMEM((rows, 128), F32)
    results = pl.pallas_call(
        functools.partial(line_kernel, n, pipes, capacity),
        out_shape=(
            pltpu.VMEM((rows, width), BF16),
            pltpu.VMEM((rows, top, fl), BF16),
            pltpu.VMEM((top, rows), BF16),
        ),
        in_specs=[hbm] * 9,
        out_specs=(vmem, vmem, vmem),
        scratch_shapes=[
            pltpu.VMEM((rows, top, fl), BF16),
            pltpu.VMEM((rows, top, fl), BF16),
            pltpu.VMEM((top, rows), jnp.int32),
            pltpu.VMEM((top, rows), jnp.int32),
            pltpu.VMEM((top, rows), BF16),
            pltpu.VMEM((top, rows), BF16),
            pltpu.VMEM((2 * fl, width), BF16),
            block,
            pltpu.VMEM((rows, width), BF16),
            pieces,
            pltpu.VMEM((2, n, 2 * slots, fl // 2), BF16),
            pltpu.VMEM((n, 8, 128), F32),
            pltpu.VMEM((2, n, rows, fl), BF16),
            pltpu.VMEM((n, chunks, rows, CHUNK), F32),
            block,
            block,
            block,
            pltpu.VMEM((2, n, rows, fl), F32),
            small,
            small,
            pieces,
            pieces,
            gate_tile,
            gate_tile,
            dma((7,)),
            dma((chunks,)),
            dma((chunks,)),
            dma,
            dma,
            dma((n,)),
            dma((n,)),
            dma((n,)),
            dma((n,)),
            dma((n, chunks)),
            dma((n, chunks)),
            dma((n, chunks)),
            dma((n, chunks)),
            dma((n, chunks)),
            dma((n, chunks)),
            dma((n,)),
            dma((n,)),
            dma((n,)),
            dma((n,)),
            dma,
            dma,
        ],
        compiler_params=pltpu.CompilerParams(
            collective_id=0, has_side_effects=True, vmem_limit_bytes=56 << 20
        ),
    )(
        forward_in[0],
        backward_in[0],
        forward_hidden[0],
        backward_hidden[0],
        forward_routes[0].T,
        backward_routes[0].T,
        forward_gates[0].T,
        backward_gates[0].T,
        down_weight[0, 0],
    )
    out, hidden_grads, gate_grads = pl.pallas_call(
        store_kernel,
        out_shape=(
            jax.ShapeDtypeStruct((rows, width), BF16),
            jax.ShapeDtypeStruct((rows, top, fl), BF16),
            jax.ShapeDtypeStruct((top, rows), BF16),
        ),
        in_specs=[vmem] * 3,
        out_specs=(hbm,) * 3,
        scratch_shapes=[dma((3,))],
    )(*(pltpu.with_memory_space_constraint(value, pltpu.VMEM) for value in results))
    return out[None], hidden_grads[None], gate_grads.T[None]


def solution(mesh):
    return jax.shard_map(
        line_body if mesh.shape["expert"] <= 4 and mesh.shape["dp"] == 2 else routed_body,
        mesh=mesh,
        in_specs=(
            P("pipe", "expert", "dp"),
            P("pipe", "expert", None),
            P("pipe", "expert", None),
            P("pipe", "expert", None, "dp"),
            P("pipe", "expert", "dp"),
            P("pipe", "expert", None),
            P("pipe", "expert", None),
            P("pipe", "expert", None, "dp"),
            P("pipe", "expert", None, "dp"),
        ),
        out_specs=(
            P("pipe", "expert", "dp"),
            P("pipe", "expert", None, "dp"),
            P("pipe", "expert", None),
        ),
        check_vma=False,
    )
```

```python
import functools
import jax
import jax.numpy as jnp
from jax import lax
from jax.experimental import pallas as pl
from jax.experimental.pallas import tpu as pltpu
from jax.sharding import PartitionSpec as P


def passed_along(value, axis, steps):
    count = lax.axis_size(axis)
    pairs = [(source, (source + steps) % count) for source in range(count)]
    return lax.ppermute(value, axis, pairs)


def route_targets(routes, capacity):
    flat_routes = routes.reshape(-1)
    places = jnp.arange(flat_routes.shape[0], dtype=jnp.int32)
    same_before = (flat_routes[:, None] == flat_routes[None, :]) & (places[None, :] < places[:, None])
    slot_pos = jnp.sum(same_before.astype(jnp.int32), axis=1)
    return flat_routes * capacity + slot_pos


def fill_slots(values, target, total):
    empty = jnp.zeros((total,) + values.shape[1:], values.dtype)
    return empty.at[target].set(values)


def routed_body(
    forward_in,
    forward_routes,
    forward_gates,
    forward_hidden,
    backward_in,
    backward_routes,
    backward_gates,
    backward_hidden,
    down_weight,
):
    owners = lax.axis_size("expert")
    tokens_here = forward_in.shape[1]
    route_count = forward_routes.shape[2]
    capacity = min(tokens_here, max(2, 3 * tokens_here * route_count // (2 * owners)))
    slot_count = owners * capacity
    inbound_forward = passed_along(forward_in, "pipe", 1)[0]
    inbound_backward = passed_along(backward_in, "pipe", -1)[0]
    target_forward = route_targets(forward_routes[0], capacity)
    target_backward = route_targets(backward_routes[0], capacity)
    weight = down_weight[0, 0]
    quarter = forward_hidden.shape[3]
    hidden_fwd, hidden_bwd = (forward_hidden[0], backward_hidden[0])
    send_fwd_hidden = fill_slots(
        hidden_fwd.reshape(tokens_here * route_count, -1), target_forward, slot_count
    )
    send_grads = fill_slots(
        jnp.repeat(inbound_backward, route_count, axis=0), target_backward, slot_count
    )
    send_bwd_hidden = fill_slots(
        hidden_bwd.reshape(tokens_here * route_count, -1), target_backward, slot_count
    )
    send_gates = fill_slots(backward_gates[0].reshape(-1), target_backward, slot_count)
    got_fwd_hidden = lax.all_to_all(
        send_fwd_hidden, "expert", split_axis=0, concat_axis=0, tiled=True
    )
    got_grads, got_bwd_hidden, got_gates = (
        lax.all_to_all(send_grads, "expert", split_axis=0, concat_axis=0, tiled=True),
        lax.all_to_all(send_bwd_hidden, "expert", split_axis=0, concat_axis=0, tiled=True),
        lax.all_to_all(send_gates, "expert", split_axis=0, concat_axis=0, tiled=True),
    )
    full_fwd, full_bwd = (
        lax.all_gather(got_fwd_hidden, "dp", axis=1, tiled=True),
        lax.all_gather(got_bwd_hidden, "dp", axis=1, tiled=True),
    )
    result_cols = jnp.dot(full_fwd, weight, preferred_element_type=jnp.float32).astype(jnp.bfloat16)
    proj_part = lax.dot_general(
        got_grads, weight, (((1,), (1,)), ((), ())), preferred_element_type=jnp.float32
    )
    projected = lax.psum_scatter(proj_part, "dp", scatter_dimension=1, tiled=True)
    outward = jnp.dot(full_bwd, weight, preferred_element_type=jnp.float32)
    gate_part = jnp.sum(got_grads.astype(jnp.float32) * outward, axis=1)
    gate_total = lax.psum(gate_part, "dp")
    hidden_grad = (got_gates.astype(jnp.float32)[:, None] * projected).astype(jnp.bfloat16)
    gate_grad = gate_total.astype(jnp.bfloat16)
    back_result = lax.all_to_all(result_cols, "expert", split_axis=0, concat_axis=0, tiled=True)
    back_hidden, back_gate = (
        lax.all_to_all(hidden_grad, "expert", split_axis=0, concat_axis=0, tiled=True),
        lax.all_to_all(gate_grad, "expert", split_axis=0, concat_axis=0, tiled=True),
    )
    picked_forward = (
        back_result[target_forward].reshape(tokens_here, route_count, -1).astype(jnp.float32)
    )
    gate_values = forward_gates[0].astype(jnp.float32)[:, :, None]
    forward_out = (
        inbound_forward.astype(jnp.float32) + jnp.sum(gate_values * picked_forward, axis=1)
    ).astype(jnp.bfloat16)
    hidden_grads = back_hidden[target_backward].reshape(tokens_here, route_count, quarter)
    gate_grads = back_gate[target_backward].reshape(tokens_here, route_count)
    return (forward_out[None], hidden_grads[None], gate_grads[None])


F32 = jnp.float32
BF16 = jnp.bfloat16
CHUNK = 1792


def line_kernel(
    n,
    pipes,
    capacity,
    fin,
    bin_,
    hf,
    hb,
    rf,
    rb,
    gf,
    gb,
    w,
    out,
    hg,
    gg,
    hfv,
    hbv,
    rfv,
    rbv,
    gfv,
    gbv,
    wv,
    ag,
    inb,
    hs,
    hrecv,
    sls,
    slr,
    hfull,
    res,
    snd,
    rlo,
    rhi,
    acc,
    ps,
    pr,
    pz,
    pret,
    gs,
    gr,
    in_sem,
    sh_s,
    sh_r,
    fi_s,
    fi_r,
    hd_s,
    hd_r,
    sl_s,
    sl_r,
    hx_s,
    hx_r,
    agu_s,
    agd_s,
    ag_r,
    rs_s,
    lo_r,
    hi_r,
    px_s,
    px_r,
    pz_s,
    pz_r,
    g_s,
    g_r,
):
    me = lax.axis_index("expert")
    pipe = lax.axis_index("pipe")
    half = lax.axis_index("dp")
    other = 1 - half
    after, before = lax.rem(pipe + 1, pipes), lax.rem(pipe + pipes - 1, pipes)
    rows, width = fin.shape
    fl = hf.shape[2]
    chunks = width // CHUNK
    early = chunks // 2
    wide = fl // 2
    low = capacity // 8 * 8
    shift_by = capacity - low
    slots = low + (8 if shift_by else 0)

    def cols(c):
        return pl.ds(pl.multiple_of(c * CHUNK, CHUNK), CHUNK)

    def remote(source, target, send, recv, **device):
        return pltpu.make_async_remote_copy(
            src_ref=source,
            dst_ref=target,
            send_sem=send,
            recv_sem=recv,
            device_id=device,
            device_id_type=pl.DeviceIdType.MESH,
        )

    def shift(c):
        return remote(bin_.at[:, cols(c)], ag.at[me, c], sh_s.at[c], sh_r.at[c], pipe=before)

    def forward_shift():
        return remote(fin, inb, fi_s, fi_r, pipe=after)

    def hidden_to(e):
        return remote(hs.at[e], hrecv.at[half, me], hd_s.at[e], hd_r.at[me], expert=e)

    def hidden_from(s):
        return remote(hs.at[s], hrecv.at[half, s], hd_s.at[s], hd_r.at[s], expert=s)

    def slots_to(e):
        return remote(sls.at[e], slr.at[me], sl_s.at[e], sl_r.at[me], expert=e)

    def slots_from(s):
        return remote(sls.at[s], slr.at[s], sl_s.at[s], sl_r.at[s], expert=s)

    def hidden_across(s):
        part = hrecv.at[half, s]
        return remote(part, part, hx_s.at[s], hx_r.at[s], dp=other)

    def gather_up(b, c):
        part = ag.at[b, c]
        return remote(part, part, agu_s.at[b, c], ag_r.at[b, c], expert=me + 1)

    def gather_down(b, c):
        part = ag.at[b, c]
        return remote(part, part, agd_s.at[b, c], ag_r.at[b, c], expert=me - 1)

    def sum_up(b, c):
        return remote(snd.at[b, c], rlo.at[b, c], rs_s.at[b, c], lo_r.at[b, c], expert=me + 1)

    def sum_down(b, c):
        return remote(snd.at[b, c], rhi.at[b, c], rs_s.at[b, c], hi_r.at[b, c], expert=me - 1)

    def proj_across(b):
        return remote(ps.at[b], pr.at[b], px_s.at[b], px_r.at[b], dp=other)

    def proj_to(b):
        return remote(pz.at[b], pret.at[me], pz_s.at[b], pz_r.at[me], expert=b)

    def proj_from(e):
        return remote(pz.at[e], pret.at[e], pz_s.at[e], pz_r.at[e], expert=e)

    def gate_across():
        return remote(gs, gr, g_s, g_r, dp=other)

    barrier = pltpu.get_barrier_semaphore()
    for device in ({"pipe": after}, {"pipe": before}, {"dp": other}):
        pl.semaphore_signal(
            barrier, inc=1, device_id=device, device_id_type=pl.DeviceIdType.MESH
        )
    for step in range(1, n):
        pl.semaphore_signal(
            barrier,
            inc=1,
            device_id={"expert": lax.rem(me + step, n)},
            device_id_type=pl.DeviceIdType.MESH,
        )

    loads = [
        pltpu.make_async_copy(source, target, in_sem.at[i])
        for i, (source, target) in enumerate(
            ((rf, rfv), (rb, rbv), (gf, gfv), (gb, gbv), (hf, hfv), (hb, hbv), (w, wv))
        )
    ]
    for load in loads:
        load.start()

    def each_chunk(action):
        lax.fori_loop(0, chunks, lambda c, _: (action(c), 0)[1], 0)

    def pack(left, right):
        if shift_by:
            both = [left[:low], left[low:] + right[:8], right[8:]]
        else:
            both = [left, right]
        both = jnp.concatenate(both, axis=0)
        return jnp.concatenate([both[:, : wide // 2], both[:, wide // 2 :]], axis=0).astype(BF16)

    def unpack(value):
        value = value.astype(F32)
        both = jnp.concatenate([value[: 2 * capacity], value[2 * capacity :]], axis=1)
        return both[:slots].astype(BF16), both[low : low + slots].astype(BF16)

    def matches(slot, at):
        return [
            jnp.where(slot + float(by) == at, 1.0, 0.0).astype(BF16) for by in (0, shift_by)
        ]

    def spread(slot_column, value):
        return jnp.concatenate(
            [
                jnp.dot(match, part, preferred_element_type=F32)
                for match, part in zip(matches(slot_column, at_lane), unpack(value))
            ],
            axis=1,
        )

    for load in loads[:4]:
        load.wait()
    fwd, bwd = rfv[...].astype(F32), rbv[...].astype(F32)
    at_row = lax.broadcasted_iota(jnp.int32, (2 * n, rows), 0)
    name = jnp.where(at_row >= n, at_row - n, at_row).astype(F32)
    named = jnp.zeros((2 * n, rows), F32)
    for k in range(2):
        route = jnp.where(at_row >= n, bwd[k : k + 1], fwd[k : k + 1])
        named = named + jnp.where(route == name, 1.0, 0.0)
    earlier = lax.broadcasted_iota(jnp.int32, (rows, rows), 0)
    earlier = jnp.where(earlier < lax.broadcasted_iota(jnp.int32, (rows, rows), 1), 1.0, 0.0)
    count = jnp.dot(named.astype(BF16), earlier.astype(BF16), preferred_element_type=F32)
    slot = jnp.where(named > 0.0, count, -64.0)
    table = jnp.concatenate(
        [fwd, gfv[...].astype(F32), bwd, gbv[...].astype(F32), slot], axis=0
    ).T
    at_slot = lax.broadcasted_iota(jnp.int32, (slots, rows), 0).astype(F32)
    at_lane = lax.broadcasted_iota(jnp.int32, (rows, slots), 1).astype(F32)
    for e in range(n):
        sls[e] = jnp.concatenate([slot[e : e + 1], slot[n + e : n + e + 1]], axis=0)
    loads[4].wait()
    compact = [jnp.zeros((n * slots, wide), F32)] * 2
    for k in range(2):
        scaled = (hfv[:, k, :].astype(F32) * table[:, 2 + k : 3 + k]).astype(BF16)
        for side, by in enumerate((0, shift_by)):
            place = jnp.concatenate(
                [
                    jnp.where(
                        (slot[e : e + 1] + float(by) == at_slot)
                        & (fwd[k : k + 1] == float(e)),
                        1.0,
                        0.0,
                    )
                    for e in range(n)
                ],
                axis=0,
            )
            compact[side] = compact[side] + jnp.dot(
                place.astype(BF16),
                scaled[:, side * wide : (side + 1) * wide],
                preferred_element_type=F32,
            )
    for e in range(n):
        hs[e] = pack(*(side[e * slots : (e + 1) * slots] for side in compact))

    pl.semaphore_wait(barrier, 3 + n - 1)

    for step in range(1, n):
        slots_to(lax.rem(me + step, n)).start()
        hidden_to(lax.rem(me + step, n)).start()
    each_chunk(lambda c: shift(c).start())
    hrecv[half, me] = hs[me]
    slr[me] = sls[me]
    hidden_across(me).start()

    def own_chunk(c):
        shift(c).wait_recv()

        @pl.when(me < n - 1)
        def _():
            gather_up(me, c).start()

        @pl.when(me > 0)
        def _():
            gather_down(me, c).start()

    each_chunk(own_chunk)
    forward_shift().start()

    for step in range(1, n):
        s = lax.rem(me + step, n)
        hidden_from(s).wait_recv()
        hidden_across(s).start()
        slots_from(s).wait_recv()

    for step in range(n):
        hidden_across(lax.rem(me + step, n)).wait_recv()
    columns = jnp.concatenate([slr[s] for s in range(n)], axis=0).T
    for s in range(n):
        for side in (half, other):
            hfull[side, s] = spread(columns[:, 2 * s : 2 * s + 1], hrecv[side, s]).astype(BF16)
    loads[6].wait()

    def expert_chunk(c):
        left = hfull[0].reshape(n * rows, fl)
        right = hfull[1].reshape(n * rows, fl)
        got = jnp.dot(left, wv[:fl, cols(c)], preferred_element_type=F32)
        got = got + jnp.dot(right, wv[fl:, cols(c)], preferred_element_type=F32)
        res[:, c] = got.reshape(n, rows, CHUNK)

    each_chunk(expert_chunk)

    def first_sums(far, c):
        @pl.when(me == 0)
        def _():
            snd[far, c] = res[far, c].astype(BF16)
            sum_up(far, c).start()

        @pl.when(me == n - 1)
        def _():
            near = n - 1 - far
            snd[near, c] = res[near, c].astype(BF16)
            sum_down(near, c).start()

    each_chunk(lambda c: first_sums(n - 1, c))

    def project(b, c):
        grads = ag[b, c]
        for part in range(2):
            got = lax.dot_general(
                grads,
                wv[part * fl : (part + 1) * fl, cols(c)],
                (((1,), (1,)), ((), ())),
                preferred_element_type=F32,
            )

            @pl.when(c == 0)
            def _():
                acc[part, b] = got

            @pl.when(c > 0)
            def _():
                acc[part, b] = acc[part, b] + got

    def to_peer(b):
        ps[b] = acc[other, b].astype(BF16)
        proj_across(b).start()

    def gathered(b):
        dense = (acc[half, b] + pr[b].astype(F32)).astype(BF16)
        return pack(
            *(
                jnp.dot(
                    match, dense[:, side * wide : (side + 1) * wide], preferred_element_type=F32
                )
                for side, match in enumerate(matches(slr[b, 1:2], at_slot))
            )
        )

    def to_source(b):
        proj_across(b).wait_recv()
        pz[b] = gathered(b)
        proj_to(b).start()

    def window(step):
        low, high = me - step, me + step
        up_to, down_to = me + n - step, me - (n - step)
        from_low, from_high = low >= 0, high < n

        def chunk(c):
            @pl.when(from_low)
            def _():
                gather_up(low, c).wait_recv()

                @pl.when(me < n - 1)
                def _():
                    gather_up(low, c).start()

            @pl.when(from_high)
            def _():
                gather_down(high, c).wait_recv()

                @pl.when(me > 0)
                def _():
                    gather_down(high, c).start()

            if 2 <= step < n - 1:
                first_sums(n - step, c)
            elif step == n - 1:

                @pl.when(c < early)
                def _():
                    first_sums(1, c)

            if step >= 2:

                @pl.when((me >= 1) & (up_to < n))
                def _():
                    sum_up(up_to, c).wait_recv()
                    snd[up_to, c] = (res[up_to, c] + rlo[up_to, c].astype(F32)).astype(BF16)
                    sum_up(up_to, c).start()

                @pl.when((me < n - 1) & (down_to >= 0))
                def _():
                    sum_down(down_to, c).wait_recv()
                    snd[down_to, c] = (res[down_to, c] + rhi[down_to, c].astype(F32)).astype(BF16)
                    sum_down(down_to, c).start()

            @pl.when(from_low)
            def _():
                project(low, c)

            @pl.when(from_high)
            def _():
                project(high, c)

            if step == 1:
                project(me, c)

        lax.fori_loop(0, early, lambda c, _: (chunk(c), 0)[1], 0)
        if step >= 2:
            hand_back(step - 1)
        lax.fori_loop(early, chunks, lambda c, _: (chunk(c), 0)[1], 0)

        @pl.when(from_low)
        def _():
            to_peer(low)

        @pl.when(from_high)
        def _():
            to_peer(high)

        if step == 1:
            to_peer(me)

    def hand_back(step):
        low, high = me - step, me + step

        @pl.when(low >= 0)
        def _():
            to_source(low)

        @pl.when(high < n)
        def _():
            to_source(high)

    for step in range(1, n):
        window(step)
    hand_back(n - 1)
    lax.fori_loop(early, chunks, lambda c, _: (first_sums(1, c), 0)[1], 0)
    proj_across(me).wait_recv()
    pret[me] = gathered(me)

    for step in range(1, n):
        proj_from(lax.rem(me + step, n)).wait_recv()
    loads[5].wait()
    spreads = [jnp.zeros((rows, fl), F32)] * 2
    for e in range(n):
        dense = spread(table[:, 8 + n + e : 9 + n + e], pret[e])
        spreads = [
            total + jnp.where(table[:, 4 + k : 5 + k] == float(e), dense, 0.0)
            for k, total in enumerate(spreads)
        ]
    lane = lax.broadcasted_iota(jnp.int32, gs.shape, 1)
    gate_sum = jnp.zeros(gs.shape, F32)
    for k, picked in enumerate(spreads):
        hg[:, k, :] = (table[:, 6 + k : 7 + k] * picked).astype(BF16)
        part = jnp.sum(hbv[:, k, :].astype(F32) * picked, axis=1, keepdims=True)
        gate_sum = gate_sum + jnp.where(lane == k, part, 0.0)
    gs[...] = gate_sum
    gate_across().start()

    forward_shift().wait_recv()

    def final_chunk(c):
        def total(value):
            out[:, cols(c)] = value.astype(BF16)

        base = inb[:, cols(c)].astype(F32) + res[me, c]

        @pl.when(me > 0)
        def _():
            sum_up(me, c).wait_recv()

        @pl.when(me < n - 1)
        def _():
            sum_down(me, c).wait_recv()

        @pl.when(me == 0)
        def _():
            total(base + rhi[me, c].astype(F32))

        @pl.when(me == n - 1)
        def _():
            total(base + rlo[me, c].astype(F32))

        @pl.when((me > 0) & (me < n - 1))
        def _():
            total(base + rlo[me, c].astype(F32) + rhi[me, c].astype(F32))

    lax.fori_loop(0, chunks - 1, lambda c, _: (final_chunk(c), 0)[1], 0)
    gate_across().wait_recv()
    gg[...] = (gs[...] + gr[...]).T[:2].astype(BF16)

    each_chunk(lambda c: shift(c).wait_send())
    forward_shift().wait_send()
    for step in range(1, n):
        e = lax.rem(me + step, n)
        hidden_to(e).wait_send()
        slots_to(e).wait_send()
        proj_to(e).wait_send()
    for b in range(n):
        hidden_across(b).wait_send()
        proj_across(b).wait_send()

        def drain(c):
            @pl.when((b <= me) & (me < n - 1))
            def _():
                gather_up(b, c).wait_send()

            @pl.when((b >= me) & (me > 0))
            def _():
                gather_down(b, c).wait_send()

            @pl.when((b < me - 1) | (b > me + 1))
            def _():
                sum_up(b, c).wait_send()

        each_chunk(drain)
    gate_across().wait_send()
    final_chunk(chunks - 1)

    def drain_last(c):
        @pl.when(me > 0)
        def _():
            sum_down(me - 1, c).wait_send()

        @pl.when(me < n - 1)
        def _():
            sum_up(me + 1, c).wait_send()

    each_chunk(drain_last)


def store_kernel(out_v, hg_v, gg_v, out, hg, gg, sems):
    copies = [
        pltpu.make_async_copy(source, target, sems.at[i])
        for i, (source, target) in enumerate(((out_v, out), (hg_v, hg), (gg_v, gg)))
    ]
    for copy in copies:
        copy.start()
    for copy in copies:
        copy.wait()


def line_body(
    forward_in,
    forward_routes,
    forward_gates,
    forward_hidden,
    backward_in,
    backward_routes,
    backward_gates,
    backward_hidden,
    down_weight,
):
    n = lax.axis_size("expert")
    pipes = lax.axis_size("pipe")
    rows, width = forward_in.shape[1:]
    top, fl = forward_hidden.shape[2:]
    chunks = width // CHUNK
    capacity = min(rows, max(2, 3 * rows * top // (2 * n)))
    dma = pltpu.SemaphoreType.DMA
    vmem = pl.BlockSpec(memory_space=pltpu.VMEM)
    hbm = pl.BlockSpec(memory_space=pl.ANY)
    block = pltpu.VMEM((n, chunks, rows, CHUNK), BF16)
    small = pltpu.VMEM((n, rows, fl), BF16)
    pieces = pltpu.VMEM((n, 4 * capacity, fl // 4), BF16)
    gate_tile = pltpu.VMEM((rows, 128), F32)
    results = pl.pallas_call(
        functools.partial(line_kernel, n, pipes, capacity),
        out_shape=(
            pltpu.VMEM((rows, width), BF16),
            pltpu.VMEM((rows, top, fl), BF16),
            pltpu.VMEM((top, rows), BF16),
        ),
        in_specs=[hbm] * 9,
        out_specs=(vmem, vmem, vmem),
        scratch_shapes=[
            pltpu.VMEM((rows, top, fl), BF16),
            pltpu.VMEM((rows, top, fl), BF16),
            pltpu.VMEM((top, rows), jnp.int32),
            pltpu.VMEM((top, rows), jnp.int32),
            pltpu.VMEM((top, rows), BF16),
            pltpu.VMEM((top, rows), BF16),
            pltpu.VMEM((2 * fl, width), BF16),
            block,
            pltpu.VMEM((rows, width), BF16),
            pieces,
            pltpu.VMEM((2, n, 4 * capacity, fl // 4), BF16),
            pltpu.VMEM((n, 2, rows), F32),
            pltpu.VMEM((n, 2, rows), F32),
            pltpu.VMEM((2, n, rows, fl), BF16),
            pltpu.VMEM((n, chunks, rows, CHUNK), F32),
            block,
            block,
            block,
            pltpu.VMEM((2, n, rows, fl), F32),
            small,
            small,
            pieces,
            pieces,
            gate_tile,
            gate_tile,
            dma((7,)),
            dma((chunks,)),
            dma((chunks,)),
            dma,
            dma,
            dma((n,)),
            dma((n,)),
            dma((n,)),
            dma((n,)),
            dma((n,)),
            dma((n,)),
            dma((n, chunks)),
            dma((n, chunks)),
            dma((n, chunks)),
            dma((n, chunks)),
            dma((n, chunks)),
            dma((n, chunks)),
            dma((n,)),
            dma((n,)),
            dma((n,)),
            dma((n,)),
            dma,
            dma,
        ],
        compiler_params=pltpu.CompilerParams(
            collective_id=0, has_side_effects=True, vmem_limit_bytes=56 << 20
        ),
    )(
        forward_in[0],
        backward_in[0],
        forward_hidden[0],
        backward_hidden[0],
        forward_routes[0].T,
        backward_routes[0].T,
        forward_gates[0].T,
        backward_gates[0].T,
        down_weight[0, 0],
    )
    out, hidden_grads, gate_grads = pl.pallas_call(
        store_kernel,
        out_shape=(
            jax.ShapeDtypeStruct((rows, width), BF16),
            jax.ShapeDtypeStruct((rows, top, fl), BF16),
            jax.ShapeDtypeStruct((top, rows), BF16),
        ),
        in_specs=[vmem] * 3,
        out_specs=(hbm,) * 3,
        scratch_shapes=[dma((3,))],
    )(*(pltpu.with_memory_space_constraint(value, pltpu.VMEM) for value in results))
    return out[None], hidden_grads[None], gate_grads.T[None]


def solution(mesh):
    return jax.shard_map(
        line_body if mesh.shape["expert"] <= 4 and mesh.shape["dp"] == 2 else routed_body,
        mesh=mesh,
        in_specs=(
            P("pipe", "expert", "dp"),
            P("pipe", "expert", None),
            P("pipe", "expert", None),
            P("pipe", "expert", None, "dp"),
            P("pipe", "expert", "dp"),
            P("pipe", "expert", None),
            P("pipe", "expert", None),
            P("pipe", "expert", None, "dp"),
            P("pipe", "expert", None, "dp"),
        ),
        out_specs=(
            P("pipe", "expert", "dp"),
            P("pipe", "expert", None, "dp"),
            P("pipe", "expert", None),
        ),
        check_vma=False,
    )
```

```python
import functools
import jax
import jax.numpy as jnp
from jax import lax
from jax.experimental import pallas as pl
from jax.experimental.pallas import tpu as pltpu
from jax.sharding import PartitionSpec as P


def passed_along(value, axis, steps):
    count = lax.axis_size(axis)
    pairs = [(source, (source + steps) % count) for source in range(count)]
    return lax.ppermute(value, axis, pairs)


def route_targets(routes, capacity):
    flat_routes = routes.reshape(-1)
    places = jnp.arange(flat_routes.shape[0], dtype=jnp.int32)
    same_before = (flat_routes[:, None] == flat_routes[None, :]) & (places[None, :] < places[:, None])
    slot_pos = jnp.sum(same_before.astype(jnp.int32), axis=1)
    return flat_routes * capacity + slot_pos


def fill_slots(values, target, total):
    empty = jnp.zeros((total,) + values.shape[1:], values.dtype)
    return empty.at[target].set(values)


def routed_body(
    forward_in,
    forward_routes,
    forward_gates,
    forward_hidden,
    backward_in,
    backward_routes,
    backward_gates,
    backward_hidden,
    down_weight,
):
    owners = lax.axis_size("expert")
    tokens_here = forward_in.shape[1]
    route_count = forward_routes.shape[2]
    capacity = min(tokens_here, max(2, 3 * tokens_here * route_count // (2 * owners)))
    slot_count = owners * capacity
    inbound_forward = passed_along(forward_in, "pipe", 1)[0]
    inbound_backward = passed_along(backward_in, "pipe", -1)[0]
    target_forward = route_targets(forward_routes[0], capacity)
    target_backward = route_targets(backward_routes[0], capacity)
    weight = down_weight[0, 0]
    quarter = forward_hidden.shape[3]
    hidden_fwd, hidden_bwd = (forward_hidden[0], backward_hidden[0])
    send_fwd_hidden = fill_slots(
        hidden_fwd.reshape(tokens_here * route_count, -1), target_forward, slot_count
    )
    send_grads = fill_slots(
        jnp.repeat(inbound_backward, route_count, axis=0), target_backward, slot_count
    )
    send_bwd_hidden = fill_slots(
        hidden_bwd.reshape(tokens_here * route_count, -1), target_backward, slot_count
    )
    send_gates = fill_slots(backward_gates[0].reshape(-1), target_backward, slot_count)
    got_fwd_hidden = lax.all_to_all(
        send_fwd_hidden, "expert", split_axis=0, concat_axis=0, tiled=True
    )
    got_grads, got_bwd_hidden, got_gates = (
        lax.all_to_all(send_grads, "expert", split_axis=0, concat_axis=0, tiled=True),
        lax.all_to_all(send_bwd_hidden, "expert", split_axis=0, concat_axis=0, tiled=True),
        lax.all_to_all(send_gates, "expert", split_axis=0, concat_axis=0, tiled=True),
    )
    full_fwd, full_bwd = (
        lax.all_gather(got_fwd_hidden, "dp", axis=1, tiled=True),
        lax.all_gather(got_bwd_hidden, "dp", axis=1, tiled=True),
    )
    result_cols = jnp.dot(full_fwd, weight, preferred_element_type=jnp.float32).astype(jnp.bfloat16)
    proj_part = lax.dot_general(
        got_grads, weight, (((1,), (1,)), ((), ())), preferred_element_type=jnp.float32
    )
    projected = lax.psum_scatter(proj_part, "dp", scatter_dimension=1, tiled=True)
    outward = jnp.dot(full_bwd, weight, preferred_element_type=jnp.float32)
    gate_part = jnp.sum(got_grads.astype(jnp.float32) * outward, axis=1)
    gate_total = lax.psum(gate_part, "dp")
    hidden_grad = (got_gates.astype(jnp.float32)[:, None] * projected).astype(jnp.bfloat16)
    gate_grad = gate_total.astype(jnp.bfloat16)
    back_result = lax.all_to_all(result_cols, "expert", split_axis=0, concat_axis=0, tiled=True)
    back_hidden, back_gate = (
        lax.all_to_all(hidden_grad, "expert", split_axis=0, concat_axis=0, tiled=True),
        lax.all_to_all(gate_grad, "expert", split_axis=0, concat_axis=0, tiled=True),
    )
    picked_forward = (
        back_result[target_forward].reshape(tokens_here, route_count, -1).astype(jnp.float32)
    )
    gate_values = forward_gates[0].astype(jnp.float32)[:, :, None]
    forward_out = (
        inbound_forward.astype(jnp.float32) + jnp.sum(gate_values * picked_forward, axis=1)
    ).astype(jnp.bfloat16)
    hidden_grads = back_hidden[target_backward].reshape(tokens_here, route_count, quarter)
    gate_grads = back_gate[target_backward].reshape(tokens_here, route_count)
    return (forward_out[None], hidden_grads[None], gate_grads[None])


F32 = jnp.float32
BF16 = jnp.bfloat16
CHUNK = 1792


def line_kernel(
    n,
    pipes,
    capacity,
    fin,
    bin_,
    hf,
    hb,
    rf,
    rb,
    gf,
    gb,
    w,
    out,
    hg,
    gg,
    hfv,
    hbv,
    rfv,
    rbv,
    gfv,
    gbv,
    wv,
    ag,
    inb,
    hs,
    hrecv,
    sls,
    slr,
    hfull,
    res,
    snd,
    rlo,
    rhi,
    acc,
    ps,
    pr,
    pz,
    pret,
    gs,
    gr,
    in_sem,
    sh_s,
    sh_r,
    fi_s,
    fi_r,
    hd_s,
    hd_r,
    sl_s,
    sl_r,
    hx_s,
    hx_r,
    agu_s,
    agd_s,
    ag_r,
    rs_s,
    lo_r,
    hi_r,
    px_s,
    px_r,
    pz_s,
    pz_r,
    g_s,
    g_r,
    in_z,
    in_dp,
    in_pipe,
):
    me = lax.axis_index("expert")
    pipe = lax.axis_index("pipe")
    half = lax.axis_index("dp")
    other = 1 - half
    after, before = lax.rem(pipe + 1, pipes), lax.rem(pipe + pipes - 1, pipes)
    rows, width = fin.shape
    fl = hf.shape[2]
    chunks = width // CHUNK
    early = chunks // 2
    wide = fl // 2
    low = capacity // 8 * 8
    shift_by = capacity - low
    slots = low + (8 if shift_by else 0)

    def cols(c):
        return pl.ds(pl.multiple_of(c * CHUNK, CHUNK), CHUNK)

    def remote(source, target, send, recv, **device):
        return pltpu.make_async_remote_copy(
            src_ref=source,
            dst_ref=target,
            send_sem=send,
            recv_sem=recv,
            device_id=device,
            device_id_type=pl.DeviceIdType.MESH,
        )

    def shift(c):
        return remote(bin_.at[:, cols(c)], ag.at[me, c], sh_s.at[c], sh_r.at[c], pipe=before)

    def forward_shift():
        return remote(fin, inb, fi_s, fi_r, pipe=after)

    def hidden_to(e):
        return remote(hs.at[e], hrecv.at[half, me], hd_s.at[e], hd_r.at[me], expert=e)

    def hidden_from(s):
        return remote(hs.at[s], hrecv.at[half, s], hd_s.at[s], hd_r.at[s], expert=s)

    def slots_to(e):
        return remote(sls.at[e], slr.at[me], sl_s.at[e], sl_r.at[me], expert=e)

    def slots_from(s):
        return remote(sls.at[s], slr.at[s], sl_s.at[s], sl_r.at[s], expert=s)

    def hidden_across(s):
        part = hrecv.at[half, s]
        return remote(part, part, hx_s.at[s], hx_r.at[s], dp=other)

    def gather_up(b, c):
        part = ag.at[b, c]
        return remote(part, part, agu_s.at[b, c], ag_r.at[b, c], expert=me + 1)

    def gather_down(b, c):
        part = ag.at[b, c]
        return remote(part, part, agd_s.at[b, c], ag_r.at[b, c], expert=me - 1)

    def sum_up(b, c):
        return remote(snd.at[b, c], rlo.at[b, c], rs_s.at[b, c], lo_r.at[b, c], expert=me + 1)

    def sum_down(b, c):
        return remote(snd.at[b, c], rhi.at[b, c], rs_s.at[b, c], hi_r.at[b, c], expert=me - 1)

    def proj_across(b):
        return remote(ps.at[b], pr.at[b], px_s.at[b], px_r.at[b], dp=other)

    def proj_to(b):
        return remote(pz.at[b], pret.at[me], pz_s.at[b], pz_r.at[me], expert=b)

    def proj_from(e):
        return remote(pz.at[e], pret.at[e], pz_s.at[e], pz_r.at[e], expert=e)

    def gate_across():
        return remote(gs, gr, g_s, g_r, dp=other)

    barrier = pltpu.get_barrier_semaphore()

    def signal(semaphore, **device):
        pl.semaphore_signal(
            semaphore, inc=1, device_id=device, device_id_type=pl.DeviceIdType.MESH
        )

    def if_true(condition, action):
        pl.when(condition)(action)

    for step in range(1, n):
        if_true(me + step < n, lambda: signal(barrier, expert=me + step))
    if_true(half == 0, lambda: signal(barrier, dp=other))
    for near in (after, before):
        if_true(near > pipe, lambda: signal(barrier, pipe=near))

    loads = [
        pltpu.make_async_copy(source, target, in_sem.at[i])
        for i, (source, target) in enumerate(
            ((rf, rfv), (rb, rbv), (gf, gfv), (gb, gbv), (hf, hfv), (hb, hbv), (w, wv))
        )
    ]
    for load in loads:
        load.start()

    def each_chunk(action):
        lax.fori_loop(0, chunks, lambda c, _: (action(c), 0)[1], 0)

    def pack(left, right):
        if shift_by:
            both = [left[:low], left[low:] + right[:8], right[8:]]
        else:
            both = [left, right]
        both = jnp.concatenate(both, axis=0)
        return jnp.concatenate([both[:, : wide // 2], both[:, wide // 2 :]], axis=0).astype(BF16)

    def unpack(value):
        value = value.astype(F32)
        both = jnp.concatenate([value[: 2 * capacity], value[2 * capacity :]], axis=1)
        return both[:slots].astype(BF16), both[low : low + slots].astype(BF16)

    def matches(slot, at):
        return [
            jnp.where(slot + float(by) == at, 1.0, 0.0).astype(BF16) for by in (0, shift_by)
        ]

    def spread(slot_column, value):
        return jnp.concatenate(
            [
                jnp.dot(match, part, preferred_element_type=F32)
                for match, part in zip(matches(slot_column, at_lane), unpack(value))
            ],
            axis=1,
        )

    lower = me + half + jnp.where(after < pipe, 1, 0) + jnp.where(before < pipe, 1, 0)
    if_true(lower > 0, lambda: pl.semaphore_wait(barrier, lower))
    for step in range(1, n):
        if_true(me - step >= 0, lambda: signal(in_z.at[me], expert=me - step))
    if_true(half == 1, lambda: signal(in_dp, dp=other))
    if_true(after < pipe, lambda: signal(in_pipe.at[0], pipe=after))
    if_true(before < pipe, lambda: signal(in_pipe.at[1], pipe=before))
    if_true(before < pipe, lambda: each_chunk(lambda c: shift(c).start()))

    def own_chunk(c):
        shift(c).wait_recv()

        @pl.when(me < n - 1)
        def _():
            gather_up(me, c).start()

        @pl.when(me > 0)
        def _():
            gather_down(me, c).start()

    beside = lax.rem(pipe, 2) == 0

    def first_own():
        if_true(me < n - 1, lambda: pl.semaphore_wait(in_z.at[me + 1], 1))
        own_chunk(0)

    if_true(beside, first_own)

    for load in loads[:4]:
        load.wait()
    fwd, bwd = rfv[...].astype(F32), rbv[...].astype(F32)
    at_row = lax.broadcasted_iota(jnp.int32, (2 * n, rows), 0)
    name = jnp.where(at_row >= n, at_row - n, at_row).astype(F32)
    named = jnp.zeros((2 * n, rows), F32)
    for k in range(2):
        route = jnp.where(at_row >= n, bwd[k : k + 1], fwd[k : k + 1])
        named = named + jnp.where(route == name, 1.0, 0.0)
    earlier = lax.broadcasted_iota(jnp.int32, (rows, rows), 0)
    earlier = jnp.where(earlier < lax.broadcasted_iota(jnp.int32, (rows, rows), 1), 1.0, 0.0)
    count = jnp.dot(named.astype(BF16), earlier.astype(BF16), preferred_element_type=F32)
    slot = jnp.where(named > 0.0, count, -64.0)
    table = jnp.concatenate(
        [fwd, gfv[...].astype(F32), bwd, gbv[...].astype(F32), slot], axis=0
    ).T
    at_slot = lax.broadcasted_iota(jnp.int32, (slots, rows), 0).astype(F32)
    at_lane = lax.broadcasted_iota(jnp.int32, (rows, slots), 1).astype(F32)
    for e in range(n):
        sls[e] = jnp.concatenate([slot[e : e + 1], slot[n + e : n + e + 1]], axis=0)
    loads[4].wait()
    compact = [jnp.zeros((n * slots, wide), F32)] * 2
    for k in range(2):
        scaled = (hfv[:, k, :].astype(F32) * table[:, 2 + k : 3 + k]).astype(BF16)
        for side, by in enumerate((0, shift_by)):
            place = jnp.concatenate(
                [
                    jnp.where(
                        (slot[e : e + 1] + float(by) == at_slot)
                        & (fwd[k : k + 1] == float(e)),
                        1.0,
                        0.0,
                    )
                    for e in range(n)
                ],
                axis=0,
            )
            compact[side] = compact[side] + jnp.dot(
                place.astype(BF16),
                scaled[:, side * wide : (side + 1) * wide],
                preferred_element_type=F32,
            )
    for e in range(n):
        hs[e] = pack(*(side[e * slots : (e + 1) * slots] for side in compact))

    def send_hidden(e):
        slots_to(e).start()
        hidden_to(e).start()

    def send_hidden_up(e, waited):
        if_true(jnp.logical_not(waited), lambda: pl.semaphore_wait(in_z.at[e], 1))
        send_hidden(e)

    def late_shift():
        pl.semaphore_wait(in_pipe.at[0], 1)
        each_chunk(lambda c: shift(c).start())

    for step in range(1, n):
        if_true(me - step >= 0, lambda: send_hidden(me - step))
    for step in range(1, n):
        if_true(me + step < n, lambda: send_hidden_up(me + step, beside & (step == 1)))
    if_true(before > pipe, late_shift)
    if_true(half == 0, lambda: pl.semaphore_wait(in_dp, 1))
    if_true(after > pipe, lambda: pl.semaphore_wait(in_pipe.at[1], 1))
    hrecv[half, me] = hs[me]
    slr[me] = sls[me]
    hidden_across(me).start()

    if_true(jnp.logical_not(beside), lambda: own_chunk(0))
    lax.fori_loop(1, chunks, lambda c, _: (own_chunk(c), 0)[1], 0)
    forward_shift().start()

    for step in range(1, n):
        s = lax.rem(me + step, n)
        hidden_from(s).wait_recv()
        hidden_across(s).start()
        slots_from(s).wait_recv()

    for step in range(n):
        hidden_across(lax.rem(me + step, n)).wait_recv()
    columns = jnp.concatenate([slr[s] for s in range(n)], axis=0).T
    for s in range(n):
        for side in (half, other):
            hfull[side, s] = spread(columns[:, 2 * s : 2 * s + 1], hrecv[side, s]).astype(BF16)
    loads[6].wait()

    def expert_chunk(c):
        left = hfull[0].reshape(n * rows, fl)
        right = hfull[1].reshape(n * rows, fl)
        got = jnp.dot(left, wv[:fl, cols(c)], preferred_element_type=F32)
        got = got + jnp.dot(right, wv[fl:, cols(c)], preferred_element_type=F32)
        res[:, c] = got.reshape(n, rows, CHUNK)

    each_chunk(expert_chunk)

    def first_sums(far, c):
        @pl.when(me == 0)
        def _():
            snd[far, c] = res[far, c].astype(BF16)
            sum_up(far, c).start()

        @pl.when(me == n - 1)
        def _():
            near = n - 1 - far
            snd[near, c] = res[near, c].astype(BF16)
            sum_down(near, c).start()

    each_chunk(lambda c: first_sums(n - 1, c))

    def project(b, c):
        grads = ag[b, c]
        for part in range(2):
            got = lax.dot_general(
                grads,
                wv[part * fl : (part + 1) * fl, cols(c)],
                (((1,), (1,)), ((), ())),
                preferred_element_type=F32,
            )

            @pl.when(c == 0)
            def _():
                acc[part, b] = got

            @pl.when(c > 0)
            def _():
                acc[part, b] = acc[part, b] + got

    def to_peer(b):
        ps[b] = acc[other, b].astype(BF16)
        proj_across(b).start()

    def gathered(b):
        dense = (acc[half, b] + pr[b].astype(F32)).astype(BF16)
        return pack(
            *(
                jnp.dot(
                    match, dense[:, side * wide : (side + 1) * wide], preferred_element_type=F32
                )
                for side, match in enumerate(matches(slr[b, 1:2], at_slot))
            )
        )

    def to_source(b):
        proj_across(b).wait_recv()
        pz[b] = gathered(b)
        proj_to(b).start()

    def window(step):
        low, high = me - step, me + step
        up_to, down_to = me + n - step, me - (n - step)
        from_low, from_high = low >= 0, high < n

        def chunk(c):
            @pl.when(from_low)
            def _():
                gather_up(low, c).wait_recv()

                @pl.when(me < n - 1)
                def _():
                    gather_up(low, c).start()

            @pl.when(from_high)
            def _():
                gather_down(high, c).wait_recv()

                @pl.when(me > 0)
                def _():
                    gather_down(high, c).start()

            if 2 <= step < n - 1:
                first_sums(n - step, c)
            elif step == n - 1:

                @pl.when(c < early)
                def _():
                    first_sums(1, c)

            if step >= 2:

                @pl.when((me >= 1) & (up_to < n))
                def _():
                    sum_up(up_to, c).wait_recv()
                    snd[up_to, c] = (res[up_to, c] + rlo[up_to, c].astype(F32)).astype(BF16)
                    sum_up(up_to, c).start()

                @pl.when((me < n - 1) & (down_to >= 0))
                def _():
                    sum_down(down_to, c).wait_recv()
                    snd[down_to, c] = (res[down_to, c] + rhi[down_to, c].astype(F32)).astype(BF16)
                    sum_down(down_to, c).start()

            @pl.when(from_low)
            def _():
                project(low, c)

            @pl.when(from_high)
            def _():
                project(high, c)

            if step == 1:
                project(me, c)

        lax.fori_loop(0, chunks, lambda c, _: (chunk(c), 0)[1], 0)

        @pl.when(from_low)
        def _():
            to_peer(low)

        @pl.when(from_high)
        def _():
            to_peer(high)

        if step == 1:
            to_peer(me)

    def hand_back(step):
        low, high = me - step, me + step

        @pl.when(low >= 0)
        def _():
            to_source(low)

        @pl.when(high < n)
        def _():
            to_source(high)

    for step in range(1, n):
        window(step)
        hand_back(step)
    lax.fori_loop(early, chunks, lambda c, _: (first_sums(1, c), 0)[1], 0)
    proj_across(me).wait_recv()
    pret[me] = gathered(me)

    for step in range(1, n):
        proj_from(lax.rem(me + step, n)).wait_recv()
    loads[5].wait()
    spreads = [jnp.zeros((rows, fl), F32)] * 2
    for e in range(n):
        dense = spread(table[:, 8 + n + e : 9 + n + e], pret[e])
        spreads = [
            total + jnp.where(table[:, 4 + k : 5 + k] == float(e), dense, 0.0)
            for k, total in enumerate(spreads)
        ]
    lane = lax.broadcasted_iota(jnp.int32, gs.shape, 1)
    gate_sum = jnp.zeros(gs.shape, F32)
    for k, picked in enumerate(spreads):
        hg[:, k, :] = (table[:, 6 + k : 7 + k] * picked).astype(BF16)
        part = jnp.sum(hbv[:, k, :].astype(F32) * picked, axis=1, keepdims=True)
        gate_sum = gate_sum + jnp.where(lane == k, part, 0.0)
    gs[...] = gate_sum
    gate_across().start()

    forward_shift().wait_recv()

    def final_chunk(c):
        def total(value):
            out[:, cols(c)] = value.astype(BF16)

        base = inb[:, cols(c)].astype(F32) + res[me, c]

        @pl.when(me > 0)
        def _():
            sum_up(me, c).wait_recv()

        @pl.when(me < n - 1)
        def _():
            sum_down(me, c).wait_recv()

        @pl.when(me == 0)
        def _():
            total(base + rhi[me, c].astype(F32))

        @pl.when(me == n - 1)
        def _():
            total(base + rlo[me, c].astype(F32))

        @pl.when((me > 0) & (me < n - 1))
        def _():
            total(base + rlo[me, c].astype(F32) + rhi[me, c].astype(F32))

    lax.fori_loop(0, chunks - 1, lambda c, _: (final_chunk(c), 0)[1], 0)
    gate_across().wait_recv()
    gg[...] = (gs[...] + gr[...]).T[:2].astype(BF16)

    each_chunk(lambda c: shift(c).wait_send())
    forward_shift().wait_send()
    for step in range(1, n):
        e = lax.rem(me + step, n)
        hidden_to(e).wait_send()
        slots_to(e).wait_send()
        proj_to(e).wait_send()
    for b in range(n):
        hidden_across(b).wait_send()
        proj_across(b).wait_send()

        def drain(c):
            @pl.when((b <= me) & (me < n - 1))
            def _():
                gather_up(b, c).wait_send()

            @pl.when((b >= me) & (me > 0))
            def _():
                gather_down(b, c).wait_send()

            @pl.when((b < me - 1) | (b > me + 1))
            def _():
                sum_up(b, c).wait_send()

        each_chunk(drain)
    gate_across().wait_send()
    final_chunk(chunks - 1)

    def drain_last(c):
        @pl.when(me > 0)
        def _():
            sum_down(me - 1, c).wait_send()

        @pl.when(me < n - 1)
        def _():
            sum_up(me + 1, c).wait_send()

    each_chunk(drain_last)


def store_kernel(out_v, hg_v, gg_v, out, hg, gg, sems):
    copies = [
        pltpu.make_async_copy(source, target, sems.at[i])
        for i, (source, target) in enumerate(((out_v, out), (hg_v, hg), (gg_v, gg)))
    ]
    for copy in copies:
        copy.start()
    for copy in copies:
        copy.wait()


def line_body(
    forward_in,
    forward_routes,
    forward_gates,
    forward_hidden,
    backward_in,
    backward_routes,
    backward_gates,
    backward_hidden,
    down_weight,
):
    n = lax.axis_size("expert")
    pipes = lax.axis_size("pipe")
    rows, width = forward_in.shape[1:]
    top, fl = forward_hidden.shape[2:]
    chunks = width // CHUNK
    capacity = min(rows, max(2, 3 * rows * top // (2 * n)))
    dma = pltpu.SemaphoreType.DMA
    vmem = pl.BlockSpec(memory_space=pltpu.VMEM)
    hbm = pl.BlockSpec(memory_space=pl.ANY)
    block = pltpu.VMEM((n, chunks, rows, CHUNK), BF16)
    small = pltpu.VMEM((n, rows, fl), BF16)
    pieces = pltpu.VMEM((n, 4 * capacity, fl // 4), BF16)
    gate_tile = pltpu.VMEM((rows, 128), F32)
    results = pl.pallas_call(
        functools.partial(line_kernel, n, pipes, capacity),
        out_shape=(
            pltpu.VMEM((rows, width), BF16),
            pltpu.VMEM((rows, top, fl), BF16),
            pltpu.VMEM((top, rows), BF16),
        ),
        in_specs=[hbm] * 9,
        out_specs=(vmem, vmem, vmem),
        scratch_shapes=[
            pltpu.VMEM((rows, top, fl), BF16),
            pltpu.VMEM((rows, top, fl), BF16),
            pltpu.VMEM((top, rows), jnp.int32),
            pltpu.VMEM((top, rows), jnp.int32),
            pltpu.VMEM((top, rows), BF16),
            pltpu.VMEM((top, rows), BF16),
            pltpu.VMEM((2 * fl, width), BF16),
            block,
            pltpu.VMEM((rows, width), BF16),
            pieces,
            pltpu.VMEM((2, n, 4 * capacity, fl // 4), BF16),
            pltpu.VMEM((n, 2, rows), F32),
            pltpu.VMEM((n, 2, rows), F32),
            pltpu.VMEM((2, n, rows, fl), BF16),
            pltpu.VMEM((n, chunks, rows, CHUNK), F32),
            block,
            block,
            block,
            pltpu.VMEM((2, n, rows, fl), F32),
            small,
            small,
            pieces,
            pieces,
            gate_tile,
            gate_tile,
            dma((7,)),
            dma((chunks,)),
            dma((chunks,)),
            dma,
            dma,
            dma((n,)),
            dma((n,)),
            dma((n,)),
            dma((n,)),
            dma((n,)),
            dma((n,)),
            dma((n, chunks)),
            dma((n, chunks)),
            dma((n, chunks)),
            dma((n, chunks)),
            dma((n, chunks)),
            dma((n, chunks)),
            dma((n,)),
            dma((n,)),
            dma((n,)),
            dma((n,)),
            dma,
            dma,
            pltpu.SemaphoreType.REGULAR((n,)),
            pltpu.SemaphoreType.REGULAR,
            pltpu.SemaphoreType.REGULAR((2,)),
        ],
        compiler_params=pltpu.CompilerParams(
            collective_id=0, has_side_effects=True, vmem_limit_bytes=56 << 20
        ),
    )(
        forward_in[0],
        backward_in[0],
        forward_hidden[0],
        backward_hidden[0],
        forward_routes[0].T,
        backward_routes[0].T,
        forward_gates[0].T,
        backward_gates[0].T,
        down_weight[0, 0],
    )
    out, hidden_grads, gate_grads = pl.pallas_call(
        store_kernel,
        out_shape=(
            jax.ShapeDtypeStruct((rows, width), BF16),
            jax.ShapeDtypeStruct((rows, top, fl), BF16),
            jax.ShapeDtypeStruct((top, rows), BF16),
        ),
        in_specs=[vmem] * 3,
        out_specs=(hbm,) * 3,
        scratch_shapes=[dma((3,))],
    )(*(pltpu.with_memory_space_constraint(value, pltpu.VMEM) for value in results))
    return out[None], hidden_grads[None], gate_grads.T[None]


def solution(mesh):
    return jax.shard_map(
        line_body if mesh.shape["expert"] <= 4 and mesh.shape["dp"] == 2 else routed_body,
        mesh=mesh,
        in_specs=(
            P("pipe", "expert", "dp"),
            P("pipe", "expert", None),
            P("pipe", "expert", None),
            P("pipe", "expert", None, "dp"),
            P("pipe", "expert", "dp"),
            P("pipe", "expert", None),
            P("pipe", "expert", None),
            P("pipe", "expert", None, "dp"),
            P("pipe", "expert", None, "dp"),
        ),
        out_specs=(
            P("pipe", "expert", "dp"),
            P("pipe", "expert", None, "dp"),
            P("pipe", "expert", None),
        ),
        check_vma=False,
    )
```

```python
import functools
import jax
import jax.numpy as jnp
from jax import lax
from jax.experimental import pallas as pl
from jax.experimental.pallas import tpu as pltpu
from jax.sharding import PartitionSpec as P


def passed_along(value, axis, steps):
    count = lax.axis_size(axis)
    pairs = [(source, (source + steps) % count) for source in range(count)]
    return lax.ppermute(value, axis, pairs)


def route_targets(routes, capacity):
    flat_routes = routes.reshape(-1)
    places = jnp.arange(flat_routes.shape[0], dtype=jnp.int32)
    same_before = (flat_routes[:, None] == flat_routes[None, :]) & (places[None, :] < places[:, None])
    slot_pos = jnp.sum(same_before.astype(jnp.int32), axis=1)
    return flat_routes * capacity + slot_pos


def fill_slots(values, target, total):
    empty = jnp.zeros((total,) + values.shape[1:], values.dtype)
    return empty.at[target].set(values)


def routed_body(
    forward_in,
    forward_routes,
    forward_gates,
    forward_hidden,
    backward_in,
    backward_routes,
    backward_gates,
    backward_hidden,
    down_weight,
):
    owners = lax.axis_size("expert")
    tokens_here = forward_in.shape[1]
    route_count = forward_routes.shape[2]
    capacity = min(tokens_here, max(2, 3 * tokens_here * route_count // (2 * owners)))
    slot_count = owners * capacity
    inbound_forward = passed_along(forward_in, "pipe", 1)[0]
    inbound_backward = passed_along(backward_in, "pipe", -1)[0]
    target_forward = route_targets(forward_routes[0], capacity)
    target_backward = route_targets(backward_routes[0], capacity)
    weight = down_weight[0, 0]
    quarter = forward_hidden.shape[3]
    hidden_fwd, hidden_bwd = (forward_hidden[0], backward_hidden[0])
    send_fwd_hidden = fill_slots(
        hidden_fwd.reshape(tokens_here * route_count, -1), target_forward, slot_count
    )
    send_grads = fill_slots(
        jnp.repeat(inbound_backward, route_count, axis=0), target_backward, slot_count
    )
    send_bwd_hidden = fill_slots(
        hidden_bwd.reshape(tokens_here * route_count, -1), target_backward, slot_count
    )
    send_gates = fill_slots(backward_gates[0].reshape(-1), target_backward, slot_count)
    got_fwd_hidden = lax.all_to_all(
        send_fwd_hidden, "expert", split_axis=0, concat_axis=0, tiled=True
    )
    got_grads, got_bwd_hidden, got_gates = (
        lax.all_to_all(send_grads, "expert", split_axis=0, concat_axis=0, tiled=True),
        lax.all_to_all(send_bwd_hidden, "expert", split_axis=0, concat_axis=0, tiled=True),
        lax.all_to_all(send_gates, "expert", split_axis=0, concat_axis=0, tiled=True),
    )
    full_fwd, full_bwd = (
        lax.all_gather(got_fwd_hidden, "dp", axis=1, tiled=True),
        lax.all_gather(got_bwd_hidden, "dp", axis=1, tiled=True),
    )
    result_cols = jnp.dot(full_fwd, weight, preferred_element_type=jnp.float32).astype(jnp.bfloat16)
    proj_part = lax.dot_general(
        got_grads, weight, (((1,), (1,)), ((), ())), preferred_element_type=jnp.float32
    )
    projected = lax.psum_scatter(proj_part, "dp", scatter_dimension=1, tiled=True)
    outward = jnp.dot(full_bwd, weight, preferred_element_type=jnp.float32)
    gate_part = jnp.sum(got_grads.astype(jnp.float32) * outward, axis=1)
    gate_total = lax.psum(gate_part, "dp")
    hidden_grad = (got_gates.astype(jnp.float32)[:, None] * projected).astype(jnp.bfloat16)
    gate_grad = gate_total.astype(jnp.bfloat16)
    back_result = lax.all_to_all(result_cols, "expert", split_axis=0, concat_axis=0, tiled=True)
    back_hidden, back_gate = (
        lax.all_to_all(hidden_grad, "expert", split_axis=0, concat_axis=0, tiled=True),
        lax.all_to_all(gate_grad, "expert", split_axis=0, concat_axis=0, tiled=True),
    )
    picked_forward = (
        back_result[target_forward].reshape(tokens_here, route_count, -1).astype(jnp.float32)
    )
    gate_values = forward_gates[0].astype(jnp.float32)[:, :, None]
    forward_out = (
        inbound_forward.astype(jnp.float32) + jnp.sum(gate_values * picked_forward, axis=1)
    ).astype(jnp.bfloat16)
    hidden_grads = back_hidden[target_backward].reshape(tokens_here, route_count, quarter)
    gate_grads = back_gate[target_backward].reshape(tokens_here, route_count)
    return (forward_out[None], hidden_grads[None], gate_grads[None])


F32 = jnp.float32
BF16 = jnp.bfloat16
CHUNK = 1792


def line_kernel(
    n,
    pipes,
    capacity,
    fin,
    bin_,
    hf,
    hb,
    rf,
    rb,
    gf,
    gb,
    w,
    out,
    hg,
    gg,
    hfv,
    hbv,
    rfv,
    rbv,
    gfv,
    gbv,
    wv,
    ag,
    inb,
    hs,
    hrecv,
    sls,
    slr,
    hfull,
    res,
    snd,
    rlo,
    rhi,
    acc,
    ps,
    pr,
    pz,
    pret,
    gs,
    gr,
    in_sem,
    sh_s,
    sh_r,
    fi_s,
    fi_r,
    hd_s,
    hd_r,
    sl_s,
    sl_r,
    hx_s,
    hx_r,
    agu_s,
    agd_s,
    ag_r,
    rs_s,
    lo_r,
    hi_r,
    px_s,
    px_r,
    pz_s,
    pz_r,
    g_s,
    g_r,
    in_z,
    in_dp,
    in_pipe,
):
    me = lax.axis_index("expert")
    pipe = lax.axis_index("pipe")
    half = lax.axis_index("dp")
    other = 1 - half
    after, before = lax.rem(pipe + 1, pipes), lax.rem(pipe + pipes - 1, pipes)
    rows, width = fin.shape
    fl = hf.shape[2]
    chunks = width // CHUNK
    early = chunks // 2
    wide = fl // 2
    low = capacity // 8 * 8
    shift_by = capacity - low
    slots = low + (8 if shift_by else 0)

    def cols(c):
        return pl.ds(pl.multiple_of(c * CHUNK, CHUNK), CHUNK)

    def remote(source, target, send, recv, **device):
        return pltpu.make_async_remote_copy(
            src_ref=source,
            dst_ref=target,
            send_sem=send,
            recv_sem=recv,
            device_id=device,
            device_id_type=pl.DeviceIdType.MESH,
        )

    def shift(c):
        return remote(bin_.at[:, cols(c)], ag.at[me, c], sh_s.at[c], sh_r.at[c], pipe=before)

    def forward_shift():
        return remote(fin, inb, fi_s, fi_r, pipe=after)

    def hidden_to(e):
        return remote(hs.at[e], hrecv.at[half, me], hd_s.at[e], hd_r.at[me], expert=e)

    def hidden_from(s):
        return remote(hs.at[s], hrecv.at[half, s], hd_s.at[s], hd_r.at[s], expert=s)

    def slots_to(e):
        return remote(sls.at[e], slr.at[me], sl_s.at[e], sl_r.at[me], expert=e)

    def slots_from(s):
        return remote(sls.at[s], slr.at[s], sl_s.at[s], sl_r.at[s], expert=s)

    def hidden_across(s):
        part = hrecv.at[half, s]
        return remote(part, part, hx_s.at[s], hx_r.at[s], dp=other)

    def gather_up(b, c):
        part = ag.at[b, c]
        return remote(part, part, agu_s.at[b, c], ag_r.at[b, c], expert=me + 1)

    def gather_down(b, c):
        part = ag.at[b, c]
        return remote(part, part, agd_s.at[b, c], ag_r.at[b, c], expert=me - 1)

    def sum_up(b, c):
        return remote(snd.at[b, c], rlo.at[b, c], rs_s.at[b, c], lo_r.at[b, c], expert=me + 1)

    def sum_down(b, c):
        return remote(snd.at[b, c], rhi.at[b, c], rs_s.at[b, c], hi_r.at[b, c], expert=me - 1)

    def proj_across(b):
        return remote(ps.at[b], pr.at[b], px_s.at[b], px_r.at[b], dp=other)

    def proj_to(b):
        return remote(pz.at[b], pret.at[me], pz_s.at[b], pz_r.at[me], expert=b)

    def proj_from(e):
        return remote(pz.at[e], pret.at[e], pz_s.at[e], pz_r.at[e], expert=e)

    def gate_across():
        return remote(gs, gr, g_s, g_r, dp=other)

    barrier = pltpu.get_barrier_semaphore()

    def signal(semaphore, **device):
        pl.semaphore_signal(
            semaphore, inc=1, device_id=device, device_id_type=pl.DeviceIdType.MESH
        )

    def if_true(condition, action):
        pl.when(condition)(action)

    for step in range(1, n):
        if_true(me + step < n, lambda: signal(barrier, expert=me + step))
    if_true(half == 0, lambda: signal(barrier, dp=other))
    for near in (after, before):
        if_true(near > pipe, lambda: signal(barrier, pipe=near))

    loads = [
        pltpu.make_async_copy(source, target, in_sem.at[i])
        for i, (source, target) in enumerate(
            ((rf, rfv), (rb, rbv), (gf, gfv), (gb, gbv), (hf, hfv), (hb, hbv), (w, wv))
        )
    ]
    for load in loads:
        load.start()

    def each_chunk(action):
        lax.fori_loop(0, chunks, lambda c, _: (action(c), 0)[1], 0)

    def pack(left, right):
        if shift_by:
            both = [left[:low], left[low:] + right[:8], right[8:]]
        else:
            both = [left, right]
        both = jnp.concatenate(both, axis=0)
        return jnp.concatenate([both[:, : wide // 2], both[:, wide // 2 :]], axis=0).astype(BF16)

    def unpack(value):
        value = value.astype(F32)
        both = jnp.concatenate([value[: 2 * capacity], value[2 * capacity :]], axis=1)
        return both[:slots].astype(BF16), both[low : low + slots].astype(BF16)

    def matches(slot, at):
        return [
            jnp.where(slot + float(by) == at, 1.0, 0.0).astype(BF16) for by in (0, shift_by)
        ]

    def spread(slot_column, value):
        return jnp.concatenate(
            [
                jnp.dot(match, part, preferred_element_type=F32)
                for match, part in zip(matches(slot_column, at_lane), unpack(value))
            ],
            axis=1,
        )

    lower = me + half + jnp.where(after < pipe, 1, 0) + jnp.where(before < pipe, 1, 0)
    if_true(lower > 0, lambda: pl.semaphore_wait(barrier, lower))
    for step in range(1, n):
        if_true(me - step >= 0, lambda: signal(in_z.at[me], expert=me - step))
    if_true(half == 1, lambda: signal(in_dp, dp=other))
    if_true(after < pipe, lambda: signal(in_pipe.at[0], pipe=after))
    if_true(before < pipe, lambda: signal(in_pipe.at[1], pipe=before))
    if_true(before < pipe, lambda: each_chunk(lambda c: shift(c).start()))

    def own_chunk(c):
        shift(c).wait_recv()

        @pl.when(me < n - 1)
        def _():
            gather_up(me, c).start()

        @pl.when(me > 0)
        def _():
            gather_down(me, c).start()

    beside = lax.rem(pipe, 2) == 0

    def first_own():
        if_true(me < n - 1, lambda: pl.semaphore_wait(in_z.at[me + 1], 1))
        own_chunk(0)

    if_true(beside, first_own)

    for load in loads[:4]:
        load.wait()
    fwd, bwd = rfv[...].astype(F32), rbv[...].astype(F32)
    at_row = lax.broadcasted_iota(jnp.int32, (2 * n, rows), 0)
    name = jnp.where(at_row >= n, at_row - n, at_row).astype(F32)
    named = jnp.zeros((2 * n, rows), F32)
    for k in range(2):
        route = jnp.where(at_row >= n, bwd[k : k + 1], fwd[k : k + 1])
        named = named + jnp.where(route == name, 1.0, 0.0)
    earlier = lax.broadcasted_iota(jnp.int32, (rows, rows), 0)
    earlier = jnp.where(earlier < lax.broadcasted_iota(jnp.int32, (rows, rows), 1), 1.0, 0.0)
    count = jnp.dot(named.astype(BF16), earlier.astype(BF16), preferred_element_type=F32)
    slot = jnp.where(named > 0.0, count, -64.0)
    table = jnp.concatenate(
        [fwd, gfv[...].astype(F32), bwd, gbv[...].astype(F32), slot], axis=0
    ).T
    at_slot = lax.broadcasted_iota(jnp.int32, (slots, rows), 0).astype(F32)
    at_lane = lax.broadcasted_iota(jnp.int32, (rows, slots), 1).astype(F32)
    for e in range(n):
        sls[e] = jnp.concatenate([slot[e : e + 1], slot[n + e : n + e + 1]], axis=0)
    loads[4].wait()
    compact = [jnp.zeros((n * slots, wide), F32)] * 2
    for k in range(2):
        scaled = (hfv[:, k, :].astype(F32) * table[:, 2 + k : 3 + k]).astype(BF16)
        for side, by in enumerate((0, shift_by)):
            place = jnp.concatenate(
                [
                    jnp.where(
                        (slot[e : e + 1] + float(by) == at_slot)
                        & (fwd[k : k + 1] == float(e)),
                        1.0,
                        0.0,
                    )
                    for e in range(n)
                ],
                axis=0,
            )
            compact[side] = compact[side] + jnp.dot(
                place.astype(BF16),
                scaled[:, side * wide : (side + 1) * wide],
                preferred_element_type=F32,
            )
    for e in range(n):
        hs[e] = pack(*(side[e * slots : (e + 1) * slots] for side in compact))

    def send_hidden(e):
        slots_to(e).start()
        hidden_to(e).start()

    def send_hidden_up(e, waited):
        if_true(jnp.logical_not(waited), lambda: pl.semaphore_wait(in_z.at[e], 1))
        send_hidden(e)

    def late_shift():
        pl.semaphore_wait(in_pipe.at[0], 1)
        each_chunk(lambda c: shift(c).start())

    for step in range(1, n):
        if_true(me - step >= 0, lambda: send_hidden(me - step))
    for step in range(1, n):
        if_true(me + step < n, lambda: send_hidden_up(me + step, beside & (step == 1)))
    if_true(before > pipe, late_shift)
    if_true(half == 0, lambda: pl.semaphore_wait(in_dp, 1))
    if_true(after > pipe, lambda: pl.semaphore_wait(in_pipe.at[1], 1))
    hrecv[half, me] = hs[me]
    slr[me] = sls[me]
    hidden_across(me).start()

    if_true(jnp.logical_not(beside), lambda: own_chunk(0))
    lax.fori_loop(1, chunks, lambda c, _: (own_chunk(c), 0)[1], 0)
    forward_shift().start()

    for step in range(1, n):
        s = lax.rem(me + step, n)
        hidden_from(s).wait_recv()
        hidden_across(s).start()
        slots_from(s).wait_recv()

    for step in range(n):
        hidden_across(lax.rem(me + step, n)).wait_recv()
    columns = jnp.concatenate([slr[s] for s in range(n)], axis=0).T
    for s in range(n):
        for side in (half, other):
            hfull[side, s] = spread(columns[:, 2 * s : 2 * s + 1], hrecv[side, s]).astype(BF16)
    loads[6].wait()

    def expert_chunk(c):
        left = hfull[0].reshape(n * rows, fl)
        right = hfull[1].reshape(n * rows, fl)
        got = jnp.dot(left, wv[:fl, cols(c)], preferred_element_type=F32)
        got = got + jnp.dot(right, wv[fl:, cols(c)], preferred_element_type=F32)
        res[:, c] = got.reshape(n, rows, CHUNK)

    each_chunk(expert_chunk)

    def first_sums(far, c):
        @pl.when(me == 0)
        def _():
            snd[far, c] = res[far, c].astype(BF16)
            sum_up(far, c).start()

        @pl.when(me == n - 1)
        def _():
            near = n - 1 - far
            snd[near, c] = res[near, c].astype(BF16)
            sum_down(near, c).start()

    each_chunk(lambda c: first_sums(n - 1, c))

    def project(b, c):
        grads = ag[b, c]
        for part in range(2):
            got = lax.dot_general(
                grads,
                wv[part * fl : (part + 1) * fl, cols(c)],
                (((1,), (1,)), ((), ())),
                preferred_element_type=F32,
            )

            @pl.when(c == 0)
            def _():
                acc[part, b] = got

            @pl.when(c > 0)
            def _():
                acc[part, b] = acc[part, b] + got

    def to_peer(b):
        ps[b] = acc[other, b].astype(BF16)
        proj_across(b).start()

    def gathered(b):
        dense = (acc[half, b] + pr[b].astype(F32)).astype(BF16)
        return pack(
            *(
                jnp.dot(
                    match, dense[:, side * wide : (side + 1) * wide], preferred_element_type=F32
                )
                for side, match in enumerate(matches(slr[b, 1:2], at_slot))
            )
        )

    def to_source(b):
        proj_across(b).wait_recv()
        pz[b] = gathered(b)
        proj_to(b).start()

    def window(step):
        low, high = me - step, me + step
        up_to, down_to = me + n - step, me - (n - step)
        from_low, from_high = low >= 0, high < n

        def chunk(c):
            @pl.when(from_high)
            def _():
                gather_down(high, c).wait_recv()

                @pl.when(me > 0)
                def _():
                    gather_down(high, c).start()

            @pl.when(from_low)
            def _():
                gather_up(low, c).wait_recv()

                @pl.when(me < n - 1)
                def _():
                    gather_up(low, c).start()

            if 2 <= step < n - 1:
                first_sums(n - step, c)
            elif step == n - 1:

                @pl.when(c < early)
                def _():
                    first_sums(1, c)

            if step >= 2:

                @pl.when((me < n - 1) & (down_to >= 0))
                def _():
                    sum_down(down_to, c).wait_recv()
                    snd[down_to, c] = (res[down_to, c] + rhi[down_to, c].astype(F32)).astype(BF16)
                    sum_down(down_to, c).start()

                @pl.when((me >= 1) & (up_to < n))
                def _():
                    sum_up(up_to, c).wait_recv()
                    snd[up_to, c] = (res[up_to, c] + rlo[up_to, c].astype(F32)).astype(BF16)
                    sum_up(up_to, c).start()

            @pl.when(from_low)
            def _():
                project(low, c)

            @pl.when(from_high)
            def _():
                project(high, c)

            if step == 1:
                project(me, c)

        lax.fori_loop(0, chunks, lambda c, _: (chunk(c), 0)[1], 0)

        @pl.when(from_low)
        def _():
            to_peer(low)

        @pl.when(from_high)
        def _():
            to_peer(high)

        if step == 1:
            to_peer(me)

    def hand_back(step):
        low, high = me - step, me + step

        @pl.when(low >= 0)
        def _():
            to_source(low)

        @pl.when(high < n)
        def _():
            to_source(high)

    for step in range(1, n):
        window(step)
        hand_back(step)
    lax.fori_loop(early, chunks, lambda c, _: (first_sums(1, c), 0)[1], 0)
    proj_across(me).wait_recv()
    pret[me] = gathered(me)

    for step in range(1, n):
        proj_from(lax.rem(me + step, n)).wait_recv()
    loads[5].wait()
    spreads = [jnp.zeros((rows, fl), F32)] * 2
    for e in range(n):
        dense = spread(table[:, 8 + n + e : 9 + n + e], pret[e])
        spreads = [
            total + jnp.where(table[:, 4 + k : 5 + k] == float(e), dense, 0.0)
            for k, total in enumerate(spreads)
        ]
    lane = lax.broadcasted_iota(jnp.int32, gs.shape, 1)
    gate_sum = jnp.zeros(gs.shape, F32)
    for k, picked in enumerate(spreads):
        hg[:, k, :] = (table[:, 6 + k : 7 + k] * picked).astype(BF16)
        part = jnp.sum(hbv[:, k, :].astype(F32) * picked, axis=1, keepdims=True)
        gate_sum = gate_sum + jnp.where(lane == k, part, 0.0)
    gs[...] = gate_sum
    gate_across().start()

    forward_shift().wait_recv()

    def final_chunk(c):
        def total(value):
            out[:, cols(c)] = value.astype(BF16)

        base = inb[:, cols(c)].astype(F32) + res[me, c]

        @pl.when(me > 0)
        def _():
            sum_up(me, c).wait_recv()

        @pl.when(me < n - 1)
        def _():
            sum_down(me, c).wait_recv()

        @pl.when(me == 0)
        def _():
            total(base + rhi[me, c].astype(F32))

        @pl.when(me == n - 1)
        def _():
            total(base + rlo[me, c].astype(F32))

        @pl.when((me > 0) & (me < n - 1))
        def _():
            total(base + rlo[me, c].astype(F32) + rhi[me, c].astype(F32))

    lax.fori_loop(0, chunks - 1, lambda c, _: (final_chunk(c), 0)[1], 0)
    gate_across().wait_recv()
    gg[...] = (gs[...] + gr[...]).T[:2].astype(BF16)

    each_chunk(lambda c: shift(c).wait_send())
    forward_shift().wait_send()
    for step in range(1, n):
        e = lax.rem(me + step, n)
        hidden_to(e).wait_send()
        slots_to(e).wait_send()
        proj_to(e).wait_send()
    for b in range(n):
        hidden_across(b).wait_send()
        proj_across(b).wait_send()

        def drain(c):
            @pl.when((b <= me) & (me < n - 1))
            def _():
                gather_up(b, c).wait_send()

            @pl.when((b >= me) & (me > 0))
            def _():
                gather_down(b, c).wait_send()

            @pl.when((b < me - 1) | (b > me + 1))
            def _():
                sum_up(b, c).wait_send()

        each_chunk(drain)
    gate_across().wait_send()
    final_chunk(chunks - 1)

    def drain_last(c):
        @pl.when(me > 0)
        def _():
            sum_down(me - 1, c).wait_send()

        @pl.when(me < n - 1)
        def _():
            sum_up(me + 1, c).wait_send()

    each_chunk(drain_last)


def store_kernel(out_v, hg_v, gg_v, out, hg, gg, sems):
    copies = [
        pltpu.make_async_copy(source, target, sems.at[i])
        for i, (source, target) in enumerate(((out_v, out), (hg_v, hg), (gg_v, gg)))
    ]
    for copy in copies:
        copy.start()
    for copy in copies:
        copy.wait()


def line_body(
    forward_in,
    forward_routes,
    forward_gates,
    forward_hidden,
    backward_in,
    backward_routes,
    backward_gates,
    backward_hidden,
    down_weight,
):
    n = lax.axis_size("expert")
    pipes = lax.axis_size("pipe")
    rows, width = forward_in.shape[1:]
    top, fl = forward_hidden.shape[2:]
    chunks = width // CHUNK
    capacity = min(rows, max(2, 3 * rows * top // (2 * n)))
    dma = pltpu.SemaphoreType.DMA
    vmem = pl.BlockSpec(memory_space=pltpu.VMEM)
    hbm = pl.BlockSpec(memory_space=pl.ANY)
    block = pltpu.VMEM((n, chunks, rows, CHUNK), BF16)
    small = pltpu.VMEM((n, rows, fl), BF16)
    pieces = pltpu.VMEM((n, 4 * capacity, fl // 4), BF16)
    gate_tile = pltpu.VMEM((rows, 128), F32)
    results = pl.pallas_call(
        functools.partial(line_kernel, n, pipes, capacity),
        out_shape=(
            pltpu.VMEM((rows, width), BF16),
            pltpu.VMEM((rows, top, fl), BF16),
            pltpu.VMEM((top, rows), BF16),
        ),
        in_specs=[hbm] * 9,
        out_specs=(vmem, vmem, vmem),
        scratch_shapes=[
            pltpu.VMEM((rows, top, fl), BF16),
            pltpu.VMEM((rows, top, fl), BF16),
            pltpu.VMEM((top, rows), jnp.int32),
            pltpu.VMEM((top, rows), jnp.int32),
            pltpu.VMEM((top, rows), BF16),
            pltpu.VMEM((top, rows), BF16),
            pltpu.VMEM((2 * fl, width), BF16),
            block,
            pltpu.VMEM((rows, width), BF16),
            pieces,
            pltpu.VMEM((2, n, 4 * capacity, fl // 4), BF16),
            pltpu.VMEM((n, 2, rows), F32),
            pltpu.VMEM((n, 2, rows), F32),
            pltpu.VMEM((2, n, rows, fl), BF16),
            pltpu.VMEM((n, chunks, rows, CHUNK), F32),
            block,
            block,
            block,
            pltpu.VMEM((2, n, rows, fl), F32),
            small,
            small,
            pieces,
            pieces,
            gate_tile,
            gate_tile,
            dma((7,)),
            dma((chunks,)),
            dma((chunks,)),
            dma,
            dma,
            dma((n,)),
            dma((n,)),
            dma((n,)),
            dma((n,)),
            dma((n,)),
            dma((n,)),
            dma((n, chunks)),
            dma((n, chunks)),
            dma((n, chunks)),
            dma((n, chunks)),
            dma((n, chunks)),
            dma((n, chunks)),
            dma((n,)),
            dma((n,)),
            dma((n,)),
            dma((n,)),
            dma,
            dma,
            pltpu.SemaphoreType.REGULAR((n,)),
            pltpu.SemaphoreType.REGULAR,
            pltpu.SemaphoreType.REGULAR((2,)),
        ],
        compiler_params=pltpu.CompilerParams(
            collective_id=0, has_side_effects=True, vmem_limit_bytes=56 << 20
        ),
    )(
        forward_in[0],
        backward_in[0],
        forward_hidden[0],
        backward_hidden[0],
        forward_routes[0].T,
        backward_routes[0].T,
        forward_gates[0].T,
        backward_gates[0].T,
        down_weight[0, 0],
    )
    out, hidden_grads, gate_grads = pl.pallas_call(
        store_kernel,
        out_shape=(
            jax.ShapeDtypeStruct((rows, width), BF16),
            jax.ShapeDtypeStruct((rows, top, fl), BF16),
            jax.ShapeDtypeStruct((top, rows), BF16),
        ),
        in_specs=[vmem] * 3,
        out_specs=(hbm,) * 3,
        scratch_shapes=[dma((3,))],
    )(*(pltpu.with_memory_space_constraint(value, pltpu.VMEM) for value in results))
    return out[None], hidden_grads[None], gate_grads.T[None]


def solution(mesh):
    return jax.shard_map(
        line_body if mesh.shape["expert"] <= 4 and mesh.shape["dp"] == 2 else routed_body,
        mesh=mesh,
        in_specs=(
            P("pipe", "expert", "dp"),
            P("pipe", "expert", None),
            P("pipe", "expert", None),
            P("pipe", "expert", None, "dp"),
            P("pipe", "expert", "dp"),
            P("pipe", "expert", None),
            P("pipe", "expert", None),
            P("pipe", "expert", None, "dp"),
            P("pipe", "expert", None, "dp"),
        ),
        out_specs=(
            P("pipe", "expert", "dp"),
            P("pipe", "expert", None, "dp"),
            P("pipe", "expert", None),
        ),
        check_vma=False,
    )
```
